32 devices in a mesh: clips: 2 (over y), space: 8 (over z, x), tm: 2 (over core).
Axes of the slice: x: 2, y: 2, z: 4, core: 2. Of those that a mesh axis runs over, the one named last changes fastest.
Arguments:
- tokens_in: bfloat16 [16, 8, 60, 1536], P(('clips', 'tm'), 'space'), parts along dimension 0, may hold values from -24 to 24
- mod_shift: float32 [3072], P('clips'), parts along dimension 0, may hold values from -3 to 3
- mod_scale: float32 [3072], P('clips'), parts along dimension 0, may hold values from -2 to 2
- mod_gate: float32 [3072], P('clips'), parts along dimension 0, may hold values from 0.5 to 1.5
- w_qkv: bfloat16 [1536, 2304], replicated, may hold values from -1 to 1, as said below
- q_gain: float32 [768], replicated, may hold values from 0.5 to 7, as said below
- k_gain: float32 [768], replicated, may hold values from 0.5 to 7, as said below
- w_out: bfloat16 [768, 1536], replicated, may hold values from -0.21875 to 0.21875
- windows: int32 [6, 2], replicated, may hold values from 1 to 3, as said below
- frame_lists: int32 [16, 6], P('clips'), parts along dimension 0, may hold values from 0 to 7, as said below
- frame_valid: int32 [16], P('clips'), parts along dimension 0, may hold values from 0 to 1, as said below
Outputs:
- mixed: bfloat16 [16, 8, 60, 1536], P(('clips', 'tm'), 'space'), parts along dimension 0
The draws below stay inside these ranges and needn't reach their ends.
There are 2 independent parts, one for each index of `clips`. The reference program is written for one: setup_inputs(seed, part) draws one part's arguments, and reference() takes and returns one part's arrays. A program takes and returns all parts, laid end to end along the dimension named above; an argument that names none is the same for every part. Nothing has to cross between parts.
Inputs may be any that keep to these rules, and one draw needn't show every extreme that they name: `w_qkv`: query, key and value columns in that order. `q_gain`: positive gains. `k_gain`: positive gains. `windows`: each entry 1 or 3; some head has 3 and 3, another head 1 and 1. `frame_lists`: row f names 6 different frames; entry 0 is f and entry 1 is (f + 4) mod 8. `frame_valid`: 1 for every frame f with f // 4 even; the other frames may be 0 or 1.
All inputs are finite; a program needn't handle non-finite values.
Results may differ from the reference program's by a relative error of at most 0.008.
Values may be sent and summed in bfloat16 or wider, within the bound.
No kernel may reach another device: no remote copies, remote signals or barrier semaphores. Data moves between devices by JAX's collectives and lax.ppermute only.
A program may use at most 128 MiB of HBM per device.

```python
import jax
import jax.numpy as jnp
from jax import lax

D = 1536
HEAD_DIM = 128
HEADS = 6
HD = 768
TT = 60
FR = 4
F = 8
TCOLS = 4
TROWS = 2
TILES = 8
KB = 6


def draw_tokens_in(key, part):
    first_key = jax.random.fold_in(key, 0)
    drawn = jnp.clip(jax.random.normal(first_key, (F, TILES, TT, D)), -6.0, 6.0)
    return drawn.astype(jnp.bfloat16)


def draw_w_qkv(key, part):
    first_key, second_key, third_key = jax.random.split(key, 3)
    query_cols = jnp.clip(jax.random.normal(first_key, (D, HD)), -4.0, 4.0) * D ** (-0.5)
    key_cols = jnp.clip(jax.random.normal(second_key, (D, HD)), -4.0, 4.0) * D ** (-0.5)
    value_cols = jnp.clip(jax.random.normal(third_key, (D, HD)), -4.0, 4.0) * D ** (-0.5)
    return jnp.concatenate([query_cols, key_cols, value_cols], axis=1).astype(jnp.bfloat16)


def gain_draw(key, salt_value):
    first_key = jax.random.fold_in(jax.random.fold_in(key, salt_value), 0)
    return jax.random.uniform(first_key, (HD,), minval=0.6, maxval=1.6).astype(jnp.float32)


def draw_q_gain(key, part):
    return gain_draw(key, 11)


def draw_k_gain(key, part):
    return gain_draw(key, 23)


def draw_windows(key, part):
    first_key, second_key = jax.random.split(key)
    window_sizes = jax.random.randint(first_key, (HEADS, 2), 0, 2) * 2 + 1
    head_order = jax.random.permutation(second_key, HEADS)
    head_ids = jnp.arange(HEADS, dtype=jnp.int32)[:, None]
    window_sizes = jnp.where(head_ids == head_order[0], 3, jnp.where(head_ids == head_order[1], 1, window_sizes))
    return window_sizes.astype(jnp.int32)


def draw_frame_lists(key, part):
    frame_ids = jnp.arange(F, dtype=jnp.int32)
    mirror = (frame_ids + FR) % F
    columns = frame_ids[None, :]
    priority = jax.random.randint(jax.random.fold_in(key, 7), (F, F), 0, 2 ** 20) * F + columns
    priority = jnp.where(columns == frame_ids[:, None], -2, priority)
    priority = jnp.where(columns == mirror[:, None], -1, priority)
    ranked = jnp.argsort(priority, axis=1, stable=True)
    return ranked[:, :KB].astype(jnp.int32)


def draw_frame_valid(key, part):
    frame_ids = jnp.arange(F, dtype=jnp.int32)
    coins = jax.random.randint(jax.random.fold_in(key, 13), (F,), 0, 10)
    kept = (frame_ids // FR % 2 == 0) | (coins < 7)
    return kept.astype(jnp.int32)


def centred(key, shape, scale, limit, kind=jnp.bfloat16):
    entries = scale * jax.random.normal(key, shape, jnp.float32)
    return jnp.clip(entries, min=-limit, max=limit).astype(kind)


def setup_inputs(seed: int = 0, part: int = 0) -> dict:
    streams_of = jax.random.split(jax.random.key(seed), 12)
    part_keys = jax.random.split(jax.random.fold_in(streams_of[11], part), 12)
    tokens_in = draw_tokens_in(jax.random.fold_in(jax.random.fold_in(streams_of[11], part), 71), part)
    mod_shift = centred(part_keys[1], (D,), 0.5, 3.0, jnp.float32)
    mod_scale = centred(part_keys[2], (D,), 0.4, 2.0, jnp.float32)
    mod_gate = jnp.clip(jax.random.uniform(part_keys[3], (D,), jnp.float32, 0.5, 1.5), 0.5, 1.5)
    w_qkv = draw_w_qkv(jax.random.fold_in(streams_of[11], 71), part)
    q_gain = draw_q_gain(jax.random.fold_in(streams_of[11], 71), part)
    k_gain = draw_k_gain(jax.random.fold_in(streams_of[11], 71), part)
    w_out = centred(streams_of[7], (HD, D), HD ** -0.5, 0.21875)
    windows = draw_windows(jax.random.fold_in(streams_of[11], 71), part)
    frame_lists = draw_frame_lists(jax.random.fold_in(jax.random.fold_in(streams_of[11], part), 71), part)
    frame_valid = draw_frame_valid(jax.random.fold_in(jax.random.fold_in(streams_of[11], part), 71), part)
    return {"tokens_in": tokens_in, "mod_shift": mod_shift, "mod_scale": mod_scale, "mod_gate": mod_gate, "w_qkv": w_qkv, "q_gain": q_gain, "k_gain": k_gain, "w_out": w_out, "windows": windows, "frame_lists": frame_lists, "frame_valid": frame_valid}


def layer_mod(tokens, shift_vec, scale_vec):
    floated = tokens.astype(jnp.float32)
    average = lax.optimization_barrier(jnp.mean(floated, axis=-1, keepdims=True))
    centered = floated - average
    variance = lax.optimization_barrier(jnp.mean(centered * centered, axis=-1, keepdims=True))
    normed = centered * lax.rsqrt(variance + 1e-06)
    return (normed * (1.0 + scale_vec) + shift_vec).astype(jnp.bfloat16)

def rms_gain(columns, gains):
    scaled = columns * lax.rsqrt(lax.optimization_barrier(jnp.mean(columns * columns, axis=-1, keepdims=True)) + 1e-06)
    return (scaled * gains).astype(jnp.bfloat16)

def frame_table(frame_lists, frame_valid):
    frame_total = frame_lists.shape[0]
    listed = jnp.any(frame_lists[:, :, None] == jnp.arange(frame_total, dtype=jnp.int32)[None, None, :], axis=1)
    return listed & (frame_valid == 1)[None, :]

def head_table(windows, exists):
    offsets = jnp.arange(9, dtype=jnp.int32)
    row_step = jnp.abs(offsets // 3 - 1)
    col_step = jnp.abs(offsets % 3 - 1)
    reaches = (windows - 1) // 2
    return exists[None, :] & (row_step[None, :] <= reaches[:, 0:1]) & (col_step[None, :] <= reaches[:, 1:2])

def reference(tokens_in, mod_shift, mod_scale, mod_gate, w_qkv, q_gain, k_gain, w_out, windows, frame_lists, frame_valid):
    frames, tile_count, tile_tokens, feature_dim = tokens_in.shape
    inner_dim = w_out.shape[0]
    modulated = layer_mod(tokens_in, mod_shift, mod_scale).reshape(-1, feature_dim)
    projected = jnp.dot(modulated, w_qkv, preferred_element_type=jnp.float32)
    queries = rms_gain(projected[:, :inner_dim], q_gain).reshape(frames, tile_count, tile_tokens, inner_dim)
    key_grid = rms_gain(projected[:, inner_dim:2 * inner_dim], k_gain).reshape(frames, TROWS, TCOLS, tile_tokens, inner_dim)
    value_grid = projected[:, 2 * inner_dim:].astype(jnp.bfloat16).reshape(frames, TROWS, TCOLS, tile_tokens, inner_dim)
    spacing = ((0, 0), (1, 1), (1, 1), (0, 0), (0, 0))
    key_padded = jnp.pad(key_grid, spacing)
    value_padded = jnp.pad(value_grid, spacing)
    inside = jnp.pad(jnp.ones((TROWS, TCOLS), dtype=bool), 1)
    frame_ok = frame_table(frame_lists, frame_valid)
    score_scale = HEAD_DIM ** (-0.5)

    def one_tile(tile_index):
        zero_index = jnp.zeros((), jnp.int32)
        tile_row = (tile_index // TCOLS).astype(jnp.int32)
        tile_col = (tile_index % TCOLS).astype(jnp.int32)
        corner = (zero_index, tile_row, tile_col, zero_index, zero_index)
        extent = (frames, 3, 3, tile_tokens, inner_dim)
        near_keys = lax.dynamic_slice(key_padded, corner, extent).reshape(frames * 9 * tile_tokens, inner_dim)
        near_values = lax.dynamic_slice(value_padded, corner, extent).reshape(frames * 9 * tile_tokens, inner_dim)
        exists = lax.dynamic_slice(inside, (tile_row, tile_col), (3, 3)).reshape(9)
        head_allow = head_table(windows, exists)
        query_rows = lax.dynamic_index_in_dim(queries, tile_index, 1, keepdims=False).reshape(frames * tile_tokens, inner_dim)
        results = []
        for head_index in range(HEADS):
            lower = head_index * HEAD_DIM
            upper = lower + HEAD_DIM
            scores = jnp.dot(query_rows[:, lower:upper], near_keys[:, lower:upper].T, preferred_element_type=jnp.float32) * score_scale
            allowed = jnp.broadcast_to(frame_ok[:, None, :, None, None] & head_allow[head_index][None, None, None, :, None], (frames, tile_tokens, frames, 9, tile_tokens)).reshape(frames * tile_tokens, frames * 9 * tile_tokens)
            row_max = lax.optimization_barrier(jnp.max(jnp.where(allowed, scores, -1e+30), axis=1, keepdims=True))
            weights = jnp.where(allowed, jnp.exp(scores - row_max), 0.0)
            totals = lax.optimization_barrier(jnp.sum(weights, axis=1, keepdims=True))
            portion = jnp.dot(weights.astype(jnp.bfloat16), near_values[:, lower:upper], preferred_element_type=jnp.float32) / totals
            results.append(portion)
        return jnp.concatenate(results, axis=1).astype(jnp.bfloat16)
    attended = lax.map(one_tile, jnp.arange(tile_count, dtype=jnp.int32))
    attended = attended.reshape(tile_count, frames, tile_tokens, inner_dim).transpose(1, 0, 2, 3).reshape(-1, inner_dim)
    branch = jnp.dot(attended, w_out, preferred_element_type=jnp.float32)
    mixed = tokens_in.reshape(-1, feature_dim).astype(jnp.float32) + mod_gate * branch
    return mixed.astype(jnp.bfloat16).reshape(frames, tile_count, tile_tokens, feature_dim)
```

```python
import functools

import jax
import jax.numpy as jnp
from jax import lax
from jax.experimental import pallas as pl
from jax.experimental.pallas import tpu as pltpu
from jax.sharding import PartitionSpec as P

HEAD_DIM = 128
NEG = -1e30
LOG2E = 1.4426950408889634
N_H, N_V, SLOT_H, SLOT_V, ORDER_H, ORDER_V = 0, 1, 8, 16, 24, 32
META = 40

VMEM = pl.BlockSpec(memory_space=pltpu.VMEM)
SMEM = pl.BlockSpec(memory_space=pltpu.SMEM)
ANY = pl.BlockSpec(memory_space=pl.ANY)


def rank_heads(windows, meta, heads):
    for column, count_at, slot_at, order_at in ((1, N_H, SLOT_H, ORDER_H), (0, N_V, SLOT_V, ORDER_V)):
        reach = [jnp.where(windows[h, column] >= 3, 1, 0) for h in range(heads)]
        total = sum(reach[1:], reach[0])
        meta[count_at] = total
        ahead, behind = jnp.int32(0), total
        for h in range(heads):
            slot = jnp.where(reach[h] == 1, ahead, behind)
            meta[slot_at + h] = slot
            meta[order_at + slot] = h
            ahead = ahead + reach[h]
            behind = behind + 1 - reach[h]


def project_kernel(
    heads, windows, tokens, shift, scale, w_qkv, q_gain, k_gain,
    meta, q_here, q_send, kv_here, kv_send, mod32, w_buf, sems,
):
    frames, _, tile_tokens, _ = tokens.shape
    inner = heads * HEAD_DIM
    half = inner // 2
    order = (2, 3, 4, 5, 0, 1)
    copies = {
        j: pltpu.make_async_copy(w_qkv.at[:, pl.ds(j * half, half)], w_buf.at[j], sems.at[j])
        for j in order
    }
    for j in order:
        copies[j].start()
    rank_heads(windows, meta, heads)
    gain_row = 1.0 + scale[...][None, :]
    shift_row = shift[...][None, :]
    for f in range(frames):
        floated = tokens[f, 0].astype(jnp.float32)
        average = jnp.mean(floated, axis=-1, keepdims=True)
        centered = floated - average
        variance = jnp.mean(centered * centered, axis=-1, keepdims=True)
        normed = centered * lax.rsqrt(variance + 1e-06)
        mod32[f * tile_tokens : (f + 1) * tile_tokens, :] = normed * gain_row + shift_row
    modulated = mod32[...].astype(jnp.bfloat16)

    def block(j):
        copies[j].wait()
        return jnp.dot(modulated, w_buf[j], preferred_element_type=jnp.float32)

    def normed_heads(first, second, gains):
        squares = jnp.sum(first * first, axis=-1, keepdims=True)
        squares = squares + jnp.sum(second * second, axis=-1, keepdims=True)
        factor = lax.rsqrt(squares * (1.0 / inner) + 1e-06)
        gains_row = gains[...][None, :]
        for h in range(heads):
            part, at = (first, h * HEAD_DIM) if h * HEAD_DIM < half else (second, h * HEAD_DIM - half)
            columns = part[:, at : at + HEAD_DIM] * factor
            yield h, (columns * gains_row[:, h * HEAD_DIM : (h + 1) * HEAD_DIM]).astype(jnp.bfloat16)

    for h, part in normed_heads(block(2), block(3), k_gain):
        kv_here[h, 0] = part
    first, second = block(4), block(5)
    for h in range(heads):
        part, at = (first, h * HEAD_DIM) if h * HEAD_DIM < half else (second, h * HEAD_DIM - half)
        kv_here[h, 1] = part[:, at : at + HEAD_DIM].astype(jnp.bfloat16)
    for i in range(kv_send.shape[0]):
        kv_send[i] = kv_here[meta[ORDER_H + i]]
    for h, part in normed_heads(block(0), block(1), q_gain):
        q_here[h] = part
    for i in range(q_send.shape[0]):
        q_send[i] = q_here[meta[ORDER_V + i]]


def attend_kernel(
    heads, lanes, meta, place, lists, valid, q_here, q_visit, kv_own, kv_own2, kv_left, kv_left2, kv_right, kv_right2,
    o_own, lse_own, o_visit, lse_visit, bias, q_all, stats,
):
    directions, slots, rows, _ = q_visit.shape
    frame_total, listed = lists.shape
    frames = frame_total // 2
    tile_tokens = rows // frames
    tile_keys = frame_total * tile_tokens
    here = place[0]
    has_left, has_right = place[1], place[2]

    key_at = lax.broadcasted_iota(jnp.int32, (1, 3 * tile_keys), 1)
    query_at = lax.broadcasted_iota(jnp.int32, (rows, 1), 0)
    group = jnp.zeros((1, 3 * tile_keys), jnp.int32)
    for j in range(1, 3 * frame_total):
        group = group + jnp.where(key_at >= j * tile_tokens, 1, 0)
    tile = jnp.where(group >= frame_total, 1, 0) + jnp.where(group >= 2 * frame_total, 1, 0)
    frame_slot = group - tile * frame_total
    absent = jnp.where((tile == 1) & (has_left == 0) | (tile == 2) & (has_right == 0), NEG, 0.0)
    full = jnp.zeros((rows, 3 * tile_keys), jnp.float32)
    for f in range(frames):
        row = jnp.full((1, 3 * tile_keys), NEG, jnp.float32)
        for s in range(frame_total):
            frame = (here * frames + s) % frame_total
            query_frame = here * frames + f
            seen = jnp.where(lists[query_frame, 0] == frame, 1, 0)
            for k in range(1, listed):
                seen = seen | jnp.where(lists[query_frame, k] == frame, 1, 0)
            seen = seen & jnp.where(valid[frame] == 1, 1, 0)
            row = jnp.where((frame_slot == s) & (seen == 1), 0.0, row)
        row = jnp.minimum(row, absent)
        inside = (query_at >= f * tile_tokens) & (query_at < (f + 1) * tile_tokens)
        full = jnp.where(inside, row, full)
    bias[...] = full
    stats[...] = jnp.zeros_like(stats)
    q_all[0:heads] = q_here[...]
    for d in range(directions):
        q_all[heads + d * slots : heads + (d + 1) * slots] = q_visit[d]

    lane = lax.broadcasted_iota(jnp.int32, (rows, lanes), 1)
    factor = HEAD_DIM**-0.5 * LOG2E

    def softmax_item(item, head, refs_slots, lane_at):
        keys = jnp.concatenate([ref[slot, 0] for ref, slot in refs_slots], axis=0)
        values = jnp.concatenate([ref[slot, 1] for ref, slot in refs_slots], axis=0)
        scores = lax.dot_general(
            q_all[item], keys, (((1,), (1,)), ((), ())), preferred_element_type=jnp.float32
        )
        scores = scores + bias[:, : keys.shape[0]]
        peak = jnp.max(scores, axis=1, keepdims=True)
        weights = jnp.exp2((scores - peak) * factor)
        total = jnp.sum(weights, axis=1, keepdims=True)
        summed = jnp.dot(weights.astype(jnp.bfloat16), values, preferred_element_type=jnp.float32)
        stats[0:rows] = jnp.where(lane == lane_at, peak * factor + jnp.log2(total), stats[0:rows])
        return summed / total

    def any_item(item, head, lane_at, store):
        slot = meta[SLOT_H + head]
        wide = slot < meta[N_H]

        @pl.when(wide)
        def _():
            store(softmax_item(
                item, head,
                [(kv_own, head), (kv_own2, head), (kv_left, slot), (kv_left2, slot), (kv_right, slot), (kv_right2, slot)],
                lane_at,
            ))

        @pl.when(jnp.logical_not(wide))
        def _():
            store(softmax_item(item, head, [(kv_own, head), (kv_own2, head)], lane_at))

    @pl.loop(0, heads)
    def _(h):
        def store(out):
            o_own[h] = out

        any_item(h, h, h, store)

    for d in range(directions):
        @pl.loop(0, meta[N_V])
        def _(i, d=d):
            def store(out):
                o_visit[d, i] = out.astype(o_visit.dtype)

            any_item(heads + d * slots + i, meta[ORDER_V + i], 16 + d * 8 + i, store)

    lse_own[...] = stats[...]
    turned = jnp.transpose(stats[...])
    for d in range(directions):
        lse_visit[d] = turned[16 + d * 8 : 24 + d * 8]


def output_kernel(
    heads, meta, place, tokens, gate, w_out, o_own, lse_own, o_back, lse_back,
    out, attended, wide, back,
):
    directions, slots, rows, _ = o_back.shape
    frames, _, tile_tokens, _ = tokens.shape
    back[...] = jnp.zeros_like(back)
    for d in range(directions):
        back[d * 8 : (d + 1) * 8] = lse_back[d]
    turned = jnp.transpose(back[...])[:rows]
    lane = lax.broadcasted_iota(jnp.int32, turned.shape, 1)
    for h in range(heads):
        slot = meta[SLOT_V + h]
        reaches = slot < meta[N_V]
        at = jnp.minimum(slot, slots - 1)
        parts = [(lse_own[0:rows, h : h + 1], o_own[h])]
        for d in range(directions):
            there = jnp.sum(jnp.where(lane == d * 8 + at, turned, 0.0), axis=1, keepdims=True)
            use = jnp.logical_and(reaches, place[3 + d] == 1)
            there = jnp.where(use, there, NEG)
            parts.append((there, jnp.where(use, o_back[d, at].astype(jnp.float32), 0.0)))
        peak = parts[0][0]
        for lse, _ in parts[1:]:
            peak = jnp.maximum(peak, lse)
        weights = [jnp.exp2(lse - peak) for lse, _ in parts]
        total = sum(weights[1:], weights[0])
        mixed = sum((w * o for w, (_, o) in zip(weights[1:], parts[1:])), weights[0] * parts[0][1])
        attended[:, h * HEAD_DIM : (h + 1) * HEAD_DIM] = (mixed / total).astype(jnp.bfloat16)
    branch = jnp.dot(attended[...], w_out[...], preferred_element_type=jnp.float32)
    wide[...] = branch * gate[...][None, :]
    for f in range(frames):
        mixed = tokens[f, 0].astype(jnp.float32) + wide[f * tile_tokens : (f + 1) * tile_tokens, :]
        out[f, 0] = mixed.astype(jnp.bfloat16)


def per_device(
    tokens_in, mod_shift, mod_scale, mod_gate, w_qkv, q_gain, k_gain, w_out, windows, frame_lists, frame_valid
):
    frames, _, tile_tokens, feature_dim = tokens_in.shape
    inner = w_out.shape[0]
    heads = windows.shape[0]
    rows = frames * tile_tokens
    slots = heads - 1
    space_size = lax.axis_size("space")
    assert lax.axis_size("tm") == 2
    tile_cols = min(8, space_size // 2)
    tile_rows = space_size // tile_cols
    bf16, f32 = jnp.bfloat16, jnp.float32

    spots = range(space_size)
    to_right = [(i, i + 1) for i in spots if i % tile_cols != tile_cols - 1]
    to_left = [(j, i) for i, j in to_right]
    down = [(i, i + tile_cols) for i in spots if i + tile_cols < space_size]
    up = [(j, i) for i, j in down]
    vertical = [down + up] if tile_rows == 2 else [down, up]
    directions = len(vertical)
    swap = [(0, 1), (1, 0)]

    position = lax.axis_index("space")
    tile_row = position // tile_cols
    tile_col = position % tile_cols
    has_partner = (
        [position >= 0] if tile_rows == 2 else [tile_row < tile_rows - 1, tile_row > 0]
    )
    place = jnp.stack(
        [lax.axis_index("tm"), tile_col > 0, tile_col < tile_cols - 1, *has_partner]
    ).astype(jnp.int32)

    meta, q_here, q_send, kv_here, kv_send = pl.pallas_call(
        functools.partial(project_kernel, heads),
        in_specs=[SMEM, VMEM, VMEM, VMEM, ANY, VMEM, VMEM],
        out_specs=[SMEM, VMEM, VMEM, VMEM, VMEM],
        out_shape=[
            jax.ShapeDtypeStruct((META,), jnp.int32),
            jax.ShapeDtypeStruct((heads, rows, HEAD_DIM), bf16),
            jax.ShapeDtypeStruct((slots, rows, HEAD_DIM), bf16),
            jax.ShapeDtypeStruct((heads, 2, rows, HEAD_DIM), bf16),
            jax.ShapeDtypeStruct((slots, 2, rows, HEAD_DIM), bf16),
        ],
        scratch_shapes=[
            pltpu.VMEM((rows, feature_dim), f32),
            pltpu.VMEM((6, feature_dim, inner // 2), bf16),
            pltpu.SemaphoreType.DMA((6,)),
        ],
        name="project",
    )(windows, tokens_in, mod_shift, mod_scale, w_qkv, q_gain, k_gain)

    kv_left = lax.ppermute(kv_send, "space", to_right)
    kv_right = lax.ppermute(kv_send, "space", to_left)
    q_visit = jnp.stack([lax.ppermute(q_send, "space", pairs) for pairs in vertical])
    kv_other = lax.ppermute(kv_here, "tm", swap)
    kv_left2 = lax.ppermute(kv_left, "tm", swap)
    kv_right2 = lax.ppermute(kv_right, "tm", swap)

    lanes = 128
    stat_rows = 256
    o_own, lse_own, o_visit, lse_visit = pl.pallas_call(
        functools.partial(attend_kernel, heads, lanes),
        in_specs=[SMEM] * 4 + [VMEM] * 8,
        out_specs=[VMEM] * 4,
        out_shape=[
            jax.ShapeDtypeStruct((heads, rows, HEAD_DIM), f32),
            jax.ShapeDtypeStruct((stat_rows, lanes), f32),
            jax.ShapeDtypeStruct((directions, slots, rows, HEAD_DIM), bf16),
            jax.ShapeDtypeStruct((directions, 8, stat_rows), f32),
        ],
        scratch_shapes=[
            pltpu.VMEM((rows, 3 * 2 * rows), f32),
            pltpu.VMEM((heads + directions * slots, rows, HEAD_DIM), bf16),
            pltpu.VMEM((stat_rows, lanes), f32),
        ],
        name="attend",
    )(meta, place, frame_lists, frame_valid, q_here, q_visit,
      kv_here, kv_other, kv_left, kv_left2, kv_right, kv_right2)

    back = [[(j, i) for i, j in pairs] for pairs in vertical]
    o_back = jnp.stack([lax.ppermute(o_visit[d], "space", back[d]) for d in range(directions)])
    lse_back = jnp.stack([lax.ppermute(lse_visit[d], "space", back[d]) for d in range(directions)])

    return pl.pallas_call(
        functools.partial(output_kernel, heads),
        in_specs=[SMEM, SMEM] + [VMEM] * 7,
        out_specs=VMEM,
        out_shape=jax.ShapeDtypeStruct(tokens_in.shape, bf16),
        scratch_shapes=[
            pltpu.VMEM((rows, inner), bf16),
            pltpu.VMEM((rows, feature_dim), f32),
            pltpu.VMEM((lanes, stat_rows), f32),
        ],
        name="output",
    )(meta, place, tokens_in, mod_gate, w_out, o_own, lse_own, o_back, lse_back)


def solution(mesh):
    in_specs = (
        P(("clips", "tm"), "space", None, None),
        P("clips"),
        P("clips"),
        P("clips"),
        P(),
        P(),
        P(),
        P(),
        P(),
        P("clips", None),
        P("clips"),
    )
    out_specs = P(("clips", "tm"), "space", None, None)
    return jax.shard_map(
        per_device, mesh=mesh, in_specs=in_specs, out_specs=out_specs, check_vma=False
    )
```

```python
import functools

import jax
import jax.numpy as jnp
from jax import lax
from jax.experimental import pallas as pl
from jax.experimental.pallas import tpu as pltpu
from jax.sharding import PartitionSpec as P


HEAD_DIM = 128
NEG = -1e30
LOG2E = 1.4426950408889634
N_H, N_V, SLOT_H, SLOT_V, ORDER_H, ORDER_V = 0, 1, 8, 16, 24, 32
META = 40

VMEM = pl.BlockSpec(memory_space=pltpu.VMEM)
SMEM = pl.BlockSpec(memory_space=pltpu.SMEM)
ANY = pl.BlockSpec(memory_space=pl.ANY)


def rank_heads(windows, meta, heads):
    for column, count_at, slot_at, order_at in ((1, N_H, SLOT_H, ORDER_H), (0, N_V, SLOT_V, ORDER_V)):
        reach = [jnp.where(windows[column, h] >= 3, 1, 0) for h in range(heads)]
        total = sum(reach[1:], reach[0])
        meta[count_at] = total
        ahead, behind = jnp.int32(0), total
        for h in range(heads):
            slot = jnp.where(reach[h] == 1, ahead, behind)
            meta[slot_at + h] = slot
            meta[order_at + slot] = h
            ahead = ahead + reach[h]
            behind = behind + 1 - reach[h]


def project_kernel(
    heads, windows, tokens, shift, scale, w_qkv, q_gain, k_gain,
    meta, q_here, q_send, kv_here, kv_send, w_buf, sems,
):
    tile_tokens, frames, _ = tokens.shape
    inner = heads * HEAD_DIM
    half = inner // 2
    order = (2, 3, 4, 5, 0, 1)
    copies = {
        j: pltpu.make_async_copy(w_qkv.at[:, pl.ds(j * half, half)], w_buf.at[j], sems.at[j])
        for j in order
    }
    for j in order:
        copies[j].start()
    rank_heads(windows, meta, heads)
    gain_row = 1.0 + scale[...][None, :]
    shift_row = shift[...][None, :]
    floated = tokens[...].astype(jnp.float32).reshape(tile_tokens * frames, -1)
    average = jnp.mean(floated, axis=-1, keepdims=True)
    centered = floated - average
    variance = jnp.mean(centered * centered, axis=-1, keepdims=True)
    normed = centered * lax.rsqrt(variance + 1e-06)
    modulated = (normed * gain_row + shift_row).astype(jnp.bfloat16)

    def block(j):
        copies[j].wait()
        return jnp.dot(modulated, w_buf[j], preferred_element_type=jnp.float32)

    def normed_heads(first, second, gains):
        squares = jnp.sum(first * first, axis=-1, keepdims=True)
        squares = squares + jnp.sum(second * second, axis=-1, keepdims=True)
        factor = lax.rsqrt(squares * (1.0 / inner) + 1e-06)
        gains_row = gains[...][None, :]
        for h in range(heads):
            part, at = (first, h * HEAD_DIM) if h * HEAD_DIM < half else (second, h * HEAD_DIM - half)
            columns = part[:, at : at + HEAD_DIM] * factor
            yield h, (columns * gains_row[:, h * HEAD_DIM : (h + 1) * HEAD_DIM]).astype(jnp.bfloat16)

    for h, part in normed_heads(block(2), block(3), k_gain):
        kv_here[h, 0] = part
    first, second = block(4), block(5)
    for h in range(heads):
        part, at = (first, h * HEAD_DIM) if h * HEAD_DIM < half else (second, h * HEAD_DIM - half)
        kv_here[h, 1] = part[:, at : at + HEAD_DIM].astype(jnp.bfloat16)
    for i in range(kv_send.shape[0]):
        kv_send[i] = kv_here[meta[ORDER_H + i]]
    for h, part in normed_heads(block(0), block(1), q_gain):
        q_here[h] = part
    for i in range(q_send.shape[0]):
        q_send[i] = q_here[meta[ORDER_V + i]]


def attend_kernel(
    heads, lanes, meta, place, lists, valid, q_here, q_visit, kv_own, kv_own2, kv_left, kv_left2, kv_right, kv_right2,
    o_own, lse_own, o_visit, lse_visit, bias, q_all, stats,
):
    directions, slots, rows, _ = q_visit.shape
    frame_total, listed = lists.shape
    frames = frame_total // 2
    tile_keys = 2 * rows
    here = place[0]
    has_left, has_right = place[1], place[2]

    key_at = lax.broadcasted_iota(jnp.int32, (1, 3 * tile_keys), 1)
    query_at = lax.broadcasted_iota(jnp.int32, (rows, 1), 0)
    part = sum(jnp.where(key_at >= j * rows, 1, 0) for j in range(1, 6))
    tile = part // 2
    frame_slot = (part - 2 * tile) * frames + lax.rem(key_at, frames)
    absent = jnp.where((tile == 1) & (has_left == 0) | (tile == 2) & (has_right == 0), NEG, 0.0)
    full = jnp.zeros((rows, 3 * tile_keys), jnp.float32)
    for f in range(frames):
        row = jnp.full((1, 3 * tile_keys), NEG, jnp.float32)
        for s in range(frame_total):
            frame = (here * frames + s) % frame_total
            query_frame = here * frames + f
            seen = jnp.where(lists[query_frame, 0] == frame, 1, 0)
            for k in range(1, listed):
                seen = seen | jnp.where(lists[query_frame, k] == frame, 1, 0)
            seen = seen & jnp.where(valid[frame] == 1, 1, 0)
            row = jnp.where((frame_slot == s) & (seen == 1), 0.0, row)
        row = jnp.minimum(row, absent)
        full = jnp.where(lax.rem(query_at, frames) == f, row, full)
    bias[...] = full
    stats[...] = jnp.zeros_like(stats)
    q_all[0:heads] = q_here[...]
    for d in range(directions):
        q_all[heads + d * slots : heads + (d + 1) * slots] = q_visit[d]

    lane = lax.broadcasted_iota(jnp.int32, (rows, lanes), 1)
    factor = HEAD_DIM**-0.5 * LOG2E

    def softmax_item(item, refs_slots, lane_at):
        keys = jnp.concatenate([ref[slot, 0] for ref, slot in refs_slots], axis=0)
        values = jnp.concatenate([ref[slot, 1] for ref, slot in refs_slots], axis=0)
        scores = lax.dot_general(
            q_all[item], keys, (((1,), (1,)), ((), ())), preferred_element_type=jnp.float32
        )
        scores = scores + bias[:, : keys.shape[0]]
        peak = jnp.max(scores, axis=1, keepdims=True)
        weights = jnp.exp2((scores - peak) * factor)
        total = jnp.sum(weights, axis=1, keepdims=True)
        summed = jnp.dot(weights.astype(jnp.bfloat16), values, preferred_element_type=jnp.float32)
        stats[0:rows] = jnp.where(lane == lane_at, peak * factor + jnp.log2(total), stats[0:rows])
        return summed / total

    def any_item(item, head, lane_at, store):
        slot = meta[SLOT_H + head]
        wide = slot < meta[N_H]

        @pl.when(wide)
        def _():
            store(softmax_item(
                item,
                [(kv_own, head), (kv_own2, head), (kv_left, slot), (kv_left2, slot), (kv_right, slot), (kv_right2, slot)],
                lane_at,
            ))

        @pl.when(jnp.logical_not(wide))
        def _():
            store(softmax_item(item, [(kv_own, head), (kv_own2, head)], lane_at))

    @pl.loop(0, heads)
    def _(h):
        def store(out):
            o_own[h] = out

        any_item(h, h, h, store)

    for d in range(directions):
        @pl.loop(0, meta[N_V])
        def _(i, d=d):
            def store(out):
                o_visit[d, i] = out.astype(o_visit.dtype)

            any_item(heads + d * slots + i, meta[ORDER_V + i], 16 + d * 8 + i, store)

    lse_own[...] = stats[...]
    turned = jnp.transpose(stats[...])
    for d in range(directions):
        lse_visit[d] = turned[16 + d * 8 : 24 + d * 8]


def output_kernel(
    heads, meta, place, tokens, gate, w_out, o_own, lse_own, o_back, lse_back,
    out, attended, back,
):
    directions, slots, rows, _ = o_back.shape
    tile_tokens, frames, _ = tokens.shape
    back[...] = jnp.zeros_like(back)
    for d in range(directions):
        back[d * 8 : (d + 1) * 8] = lse_back[d]
    turned = jnp.transpose(back[...])[:rows]
    lane = lax.broadcasted_iota(jnp.int32, turned.shape, 1)
    for h in range(heads):
        slot = meta[SLOT_V + h]
        reaches = slot < meta[N_V]
        at = jnp.minimum(slot, slots - 1)
        parts = [(lse_own[0:rows, h : h + 1], o_own[h])]
        for d in range(directions):
            there = jnp.sum(jnp.where(lane == d * 8 + at, turned, 0.0), axis=1, keepdims=True)
            use = jnp.logical_and(reaches, place[3 + d] == 1)
            there = jnp.where(use, there, NEG)
            parts.append((there, jnp.where(use, o_back[d, at].astype(jnp.float32), 0.0)))
        peak = parts[0][0]
        for lse, _ in parts[1:]:
            peak = jnp.maximum(peak, lse)
        weights = [jnp.exp2(lse - peak) for lse, _ in parts]
        total = sum(weights[1:], weights[0])
        mixed = sum((w * o for w, (_, o) in zip(weights[1:], parts[1:])), weights[0] * parts[0][1])
        attended[:, h * HEAD_DIM : (h + 1) * HEAD_DIM] = (mixed / total).astype(jnp.bfloat16)
    branch = jnp.dot(attended[...], w_out[...], preferred_element_type=jnp.float32)
    branch = (branch * gate[...][None, :]).reshape(tile_tokens, frames, -1)
    out[...] = (tokens[...].astype(jnp.float32) + branch).astype(jnp.bfloat16)


def per_device(
    tokens_in, mod_shift, mod_scale, mod_gate, w_qkv, q_gain, k_gain, w_out, windows, frame_lists, frame_valid
):
    frames, _, tile_tokens, feature_dim = tokens_in.shape
    inner = w_out.shape[0]
    heads = windows.shape[0]
    rows = frames * tile_tokens
    slots = heads - 1
    space_size = lax.axis_size("space")
    assert lax.axis_size("tm") == 2
    tile_cols = min(8, space_size // 2)
    tile_rows = space_size // tile_cols
    bf16, f32 = jnp.bfloat16, jnp.float32
    tokens = jnp.transpose(tokens_in[:, 0], (1, 0, 2))

    spots = range(space_size)
    to_right = [(i, i + 1) for i in spots if i % tile_cols != tile_cols - 1]
    to_left = [(j, i) for i, j in to_right]
    down = [(i, i + tile_cols) for i in spots if i + tile_cols < space_size]
    up = [(j, i) for i, j in down]
    vertical = [down + up] if tile_rows == 2 else [down, up]
    directions = len(vertical)
    swap = [(0, 1), (1, 0)]

    position = lax.axis_index("space")
    tile_row = position // tile_cols
    tile_col = position % tile_cols
    has_partner = (
        [position >= 0] if tile_rows == 2 else [tile_row < tile_rows - 1, tile_row > 0]
    )
    place = jnp.stack(
        [lax.axis_index("tm"), tile_col > 0, tile_col < tile_cols - 1, *has_partner]
    ).astype(jnp.int32)

    meta, q_here, q_send, kv_here, kv_send = pl.pallas_call(
        functools.partial(project_kernel, heads),
        in_specs=[SMEM, VMEM, VMEM, VMEM, ANY, VMEM, VMEM],
        out_specs=[SMEM, VMEM, VMEM, VMEM, VMEM],
        out_shape=[
            jax.ShapeDtypeStruct((META,), jnp.int32),
            jax.ShapeDtypeStruct((heads, rows, HEAD_DIM), bf16),
            jax.ShapeDtypeStruct((slots, rows, HEAD_DIM), bf16),
            jax.ShapeDtypeStruct((heads, 2, rows, HEAD_DIM), bf16),
            jax.ShapeDtypeStruct((slots, 2, rows, HEAD_DIM), bf16),
        ],
        scratch_shapes=[
            pltpu.VMEM((6, feature_dim, inner // 2), bf16),
            pltpu.SemaphoreType.DMA((6,)),
        ],
        name="project",
    )(windows.T, tokens, mod_shift, mod_scale, w_qkv, q_gain, k_gain)

    back = [[(j, i) for i, j in pairs] for pairs in vertical]
    lanes = 128
    stat_rows = 256

    def along_row(sent, *operands):
        return row_step(sent, *operands)

    def row_step(sent, kv_send, kv_here, q_send, q_here, meta):
        kv_send = kv_send[:sent]
        q_visit = jnp.stack([lax.ppermute(q_send, "space", pairs) for pairs in vertical])
        kv_left = lax.ppermute(kv_send, "space", to_right)
        kv_right = lax.ppermute(kv_send, "space", to_left)
        kv_other = lax.ppermute(kv_here, "tm", swap)
        kv_left2 = lax.ppermute(kv_left, "tm", swap)
        kv_right2 = lax.ppermute(kv_right, "tm", swap)
        return pl.pallas_call(
            functools.partial(attend_kernel, heads, lanes),
            in_specs=[SMEM] * 4 + [VMEM] * 8,
            out_specs=[VMEM] * 4,
            out_shape=[
                jax.ShapeDtypeStruct((heads, rows, HEAD_DIM), f32),
                jax.ShapeDtypeStruct((stat_rows, lanes), f32),
                jax.ShapeDtypeStruct((directions, slots, rows, HEAD_DIM), bf16),
                jax.ShapeDtypeStruct((directions, 8, stat_rows), f32),
            ],
            scratch_shapes=[
                pltpu.VMEM((rows, 3 * 2 * rows), f32),
                pltpu.VMEM((heads + directions * slots, rows, HEAD_DIM), bf16),
                pltpu.VMEM((stat_rows, lanes), f32),
            ],
            name="attend",
        )(meta, place, frame_lists, frame_valid, q_here, q_visit,
          kv_here, kv_other, kv_left, kv_left2, kv_right, kv_right2)

    o_own, lse_own, o_visit, lse_visit = lax.switch(
        meta[N_H] - 1,
        [functools.partial(along_row, n) for n in range(1, slots + 1)],
        kv_send, kv_here, q_send, q_here, meta,
    )

    def between_rows(sent, o_own, lse_own, o_visit, lse_visit, meta):
        o_back = jnp.stack([lax.ppermute(o_visit[d, :sent], "space", back[d]) for d in range(directions)])
        lse_back = jnp.stack([lax.ppermute(lse_visit[d], "space", back[d]) for d in range(directions)])
        return pl.pallas_call(
            functools.partial(output_kernel, heads),
            in_specs=[SMEM, SMEM] + [VMEM] * 7,
            out_specs=VMEM,
            out_shape=jax.ShapeDtypeStruct(tokens.shape, bf16),
            scratch_shapes=[
                pltpu.VMEM((rows, inner), bf16),
                pltpu.VMEM((lanes, stat_rows), f32),
            ],
            name="output",
        )(meta, place, tokens, mod_gate, w_out, o_own, lse_own, o_back, lse_back)

    mixed = lax.switch(
        meta[N_V] - 1,
        [functools.partial(between_rows, n) for n in range(1, slots + 1)],
        o_own, lse_own, o_visit, lse_visit, meta,
    )
    return jnp.transpose(mixed, (1, 0, 2))[:, None]


def solution(mesh):
    in_specs = (
        P(("clips", "tm"), "space", None, None),
        P("clips"),
        P("clips"),
        P("clips"),
        P(),
        P(),
        P(),
        P(),
        P(),
        P("clips", None),
        P("clips"),
    )
    out_specs = P(("clips", "tm"), "space", None, None)
    return jax.shard_map(
        per_device, mesh=mesh, in_specs=in_specs, out_specs=out_specs, check_vma=False
    )
```

```python
import functools

import jax
import jax.numpy as jnp
from jax import lax
from jax.experimental import pallas as pl
from jax.experimental.pallas import tpu as pltpu
from jax.sharding import PartitionSpec as P


HEAD_DIM = 128
NEG = -1e30
LOG2E = 1.4426950408889634
N_H, N_V, N_BOTH, SLOT_H, SLOT_V, ORDER_H, ORDER_V = 0, 1, 2, 8, 16, 24, 32
META = 40

VMEM = pl.BlockSpec(memory_space=pltpu.VMEM)
SMEM = pl.BlockSpec(memory_space=pltpu.SMEM)
HBM = pl.BlockSpec(memory_space=pltpu.HBM)


def params(mebibytes):
    return pltpu.CompilerParams(vmem_limit_bytes=mebibytes << 20)


def rank_heads(windows, meta, heads):
    wide = [jnp.where(windows[1, h] >= 3, 1, 0) for h in range(heads)]
    tall = [jnp.where(windows[0, h] >= 3, 1, 0) for h in range(heads)]
    both = [w * t for w, t in zip(wide, tall)]
    meta[N_H], meta[N_V], meta[N_BOTH] = sum(wide), sum(tall), sum(both)
    for classes, slot_at, order_at in (
        ([1 - w for w in wide], SLOT_H, ORDER_H),
        ([2 - t - b for t, b in zip(tall, both)], SLOT_V, ORDER_V),
    ):
        for h in range(heads):
            slot = sum(
                jnp.where((classes[o] < classes[h]) | ((classes[o] == classes[h]) & (o < h)), 1, 0)
                for o in range(heads) if o != h
            )
            meta[slot_at + h] = slot
            meta[order_at + slot] = h


def project_kernel(
    heads, windows_at, tokens_at, shift_at, scale_at, w_qkv, q_gain_at, k_gain_at,
    meta, q_here, q_send, kv_here,
    windows, tokens, shift, scale, q_gain, k_gain, modulated, w_buf, small_sems, sems,
):
    tile_tokens, frames, _ = tokens.shape
    inner = heads * HEAD_DIM
    queries, keys, values = 0, 1, 2
    small = [
        pltpu.make_async_copy(there, ref, small_sems.at[i])
        for i, (there, ref) in enumerate((
            (tokens_at, tokens), (shift_at, shift), (scale_at, scale),
            (windows_at, windows), (k_gain_at, k_gain), (q_gain_at, q_gain),
        ))
    ]
    blocks = {
        j: pltpu.make_async_copy(w_qkv.at[:, pl.ds(j * inner, inner)], w_buf.at[j], sems.at[j])
        for j in (keys, values, queries)
    }
    for copy in (*small, *blocks.values()):
        copy.start()
    for copy in small:
        copy.wait()
    rank_heads(windows, meta, heads)
    gain_row = 1.0 + scale[...][None, :]
    shift_row = shift[...][None, :]
    step = 4
    for t in range(0, tile_tokens, step):
        floated = tokens[t : t + step].astype(jnp.float32).reshape(step * frames, -1)
        average = jnp.mean(floated, axis=-1, keepdims=True)
        centered = floated - average
        variance = jnp.mean(centered * centered, axis=-1, keepdims=True)
        normed = centered * lax.rsqrt(variance + 1e-06)
        modulated[t * frames : (t + step) * frames] = (normed * gain_row + shift_row).astype(jnp.bfloat16)

    def block(j):
        blocks[j].wait()
        return jnp.dot(modulated[...], w_buf[j], preferred_element_type=jnp.float32)

    def normed_heads(columns, gains):
        squares = jnp.sum(columns * columns, axis=-1, keepdims=True)
        factor = lax.rsqrt(squares * (1.0 / inner) + 1e-06)
        gains_row = gains[...][None, :]
        for h in range(heads):
            at = slice(h * HEAD_DIM, (h + 1) * HEAD_DIM)
            yield h, (columns[:, at] * factor * gains_row[:, at]).astype(jnp.bfloat16)

    for h, part in normed_heads(block(keys), k_gain):
        kv_here[h, 0] = part
    columns = block(values)
    for h in range(heads):
        kv_here[h, 1] = columns[:, h * HEAD_DIM : (h + 1) * HEAD_DIM].astype(jnp.bfloat16)
    for h, part in normed_heads(block(queries), q_gain):
        q_here[h] = part
    for i in range(q_send.shape[0]):
        q_send[i] = q_here[meta[ORDER_V + i]]


def pack_kernel(meta, kv_here, k_send, v_send):
    for i in range(k_send.shape[0]):
        k_send[i] = kv_here[meta[ORDER_H + i], 0]
        v_send[i] = kv_here[meta[ORDER_H + i], 1]


def softmax_over(query, parts):
    factor = HEAD_DIM**-0.5 * LOG2E
    scores = []
    for pieces, bias in parts:
        keys = jnp.concatenate([key() for key, _ in pieces], axis=0)
        part = lax.dot_general(query, keys, (((1,), (1,)), ((), ())), preferred_element_type=jnp.float32)
        scores.append(part + bias[...])
    peak = functools.reduce(jnp.maximum, [jnp.max(part, axis=1, keepdims=True) for part in scores])
    total, summed = 0.0, 0.0
    for part, (pieces, _) in zip(scores, parts):
        values = jnp.concatenate([value() for _, value in pieces], axis=0)
        weights = jnp.exp2((part - peak) * factor)
        total = total + jnp.sum(weights, axis=1, keepdims=True)
        summed = summed + jnp.dot(weights.astype(jnp.bfloat16), values, preferred_element_type=jnp.float32)
    return summed / total, peak * factor + jnp.log2(total)


def own_pieces(kv_refs, head):
    return [(lambda ref=ref: ref[head, 0], lambda ref=ref: ref[head, 1]) for ref in kv_refs]


def near_pieces(refs, slot):
    return [(lambda k=k: k[slot], lambda v=v: v[slot]) for k, v in refs]


def own_tile_kernel(
    heads, place, lists, valid, q_here, kv_own, kv_own2, o_own, lse_own, bias_own, bias_near
):
    rows = q_here.shape[1]
    frame_total, listed = lists.shape
    frames = frame_total // 2
    here = place[0]
    key_at = lax.broadcasted_iota(jnp.int32, (1, 4 * rows), 1)
    query_at = lax.broadcasted_iota(jnp.int32, (rows, 1), 0)
    part = sum(jnp.where(key_at >= j * rows, 1, 0) for j in range(1, 4))
    frame_slot = (part & 1) * frames + lax.rem(key_at, frames)
    absent = jnp.where((part >= 2) & (place[1] == 0), NEG, 0.0)
    seen_rows = []
    for f in range(frames):
        row = jnp.full((1, 4 * rows), NEG, jnp.float32)
        for s in range(frame_total):
            frame = (here * frames + s) % frame_total
            query_frame = here * frames + f
            seen = jnp.where(lists[query_frame, 0] == frame, 1, 0)
            for k in range(1, listed):
                seen = seen | jnp.where(lists[query_frame, k] == frame, 1, 0)
            seen = seen & jnp.where(valid[frame] == 1, 1, 0)
            row = jnp.where((frame_slot == s) & (seen == 1), 0.0, row)
        seen_rows.append(row)
    query_frame = lax.rem(query_at, frames)

    def spread(picked):
        full = jnp.broadcast_to(picked[0], (rows, picked[0].shape[1]))
        for f in range(1, frames):
            full = jnp.where(query_frame == f, picked[f], full)
        return full

    bias_own[...] = spread([row[:, : 2 * rows] for row in seen_rows])
    bias_near[...] = spread([jnp.minimum(row, absent) for row in seen_rows])
    lane = lax.broadcasted_iota(jnp.int32, lse_own.shape, 1)
    lse_own[...] = jnp.zeros_like(lse_own)

    @pl.loop(0, heads)
    def _(h):
        out, lse = softmax_over(q_here[h], [(own_pieces((kv_own, kv_own2), h), bias_own)])
        o_own[h] = out
        lse_own[...] = jnp.where(lane == h, lse, lse_own[...])


def attend_kernel(
    meta, q_here, q_visit, kv_own, kv_own2, k_pair, v_pair, k_pair2, v_pair2, k_far, v_far, k_far2, v_far2,
    bias_own, bias_near, o_near, lse_near, o_visit, lse_visit, stats,
):
    directions, _, rows, _ = q_visit.shape
    lane = lax.broadcasted_iota(jnp.int32, (rows, stats.shape[1]), 1)
    stats[...] = jnp.zeros_like(stats)
    sent = k_pair.shape[0]

    def near(slot):
        refs = ((k_pair, v_pair), (k_pair2, v_pair2), (k_far, v_far), (k_far2, v_far2))
        return near_pieces(refs, slot), bias_near

    def own(head):
        return own_pieces((kv_own, kv_own2), head), bias_own

    def keep(lane_at, lse):
        stats[0:rows] = jnp.where(lane == lane_at, lse, stats[0:rows])

    for i in range(sent):
        out, lse = softmax_over(q_here[meta[ORDER_H + i]], [near(i)])
        o_near[i] = out
        keep(i, lse)

    for d in range(directions):
        @pl.loop(0, meta[N_BOTH])
        def _(i, d=d):
            head = meta[ORDER_V + i]
            out, lse = softmax_over(q_visit[d, i], [near(meta[SLOT_H + head]), own(head)])
            o_visit[d, i] = out.astype(o_visit.dtype)
            keep(16 + d * 8 + i, lse)

        @pl.loop(meta[N_BOTH], meta[N_V])
        def _(i, d=d):
            out, lse = softmax_over(q_visit[d, i], [own(meta[ORDER_V + i])])
            o_visit[d, i] = out.astype(o_visit.dtype)
            keep(16 + d * 8 + i, lse)

    lse_near[...] = stats[0:rows]
    turned = jnp.transpose(stats[...])
    for d in range(directions):
        lse_visit[d] = turned[16 + d * 8 : 24 + d * 8]


def merge(parts):
    peak = functools.reduce(jnp.maximum, [lse for lse, _ in parts])
    weights = [jnp.exp2(lse - peak) for lse, _ in parts]
    total = sum(weights[1:], weights[0])
    mixed = sum((w * o for w, (_, o) in zip(weights[1:], parts[1:])), weights[0] * parts[0][1])
    return mixed / total, peak + jnp.log2(total)


def pick_lane(table, at):
    lane = lax.broadcasted_iota(jnp.int32, table.shape, 1)
    return jnp.sum(jnp.where(lane == at, table, 0.0), axis=1, keepdims=True)


def row_kernel(heads, meta, o_own, lse_own, o_near, lse_near, o_row, lse_row):
    lane = lax.broadcasted_iota(jnp.int32, lse_row.shape, 1)
    own, near = lse_own[...], lse_near[...]
    merged = own
    for h in range(heads):
        slot = meta[SLOT_H + h]
        use = slot < meta[N_H]
        at = jnp.minimum(slot, o_near.shape[0] - 1)
        there = jnp.where(use, pick_lane(near, at), NEG)
        result, lse = merge([(own[:, h : h + 1], o_own[h]), (there, jnp.where(use, o_near[at], 0.0))])
        o_row[h] = result
        merged = jnp.where(lane == h, lse, merged)
    lse_row[...] = merged


def output_kernel(
    heads, meta, place, tokens, gate, w_out, o_row, lse_row, o_back, lse_back,
    out, attended, back, staged, sems,
):
    directions, slots, rows, _ = o_back.shape
    tile_tokens, frames, _ = tokens.shape
    back[...] = jnp.zeros_like(back)
    for d in range(directions):
        back[d * 8 : (d + 1) * 8] = lse_back[d]
    turned = jnp.transpose(back[...])[:rows]
    for h in range(heads):
        parts = [(lse_row[:, h : h + 1], o_row[h])]
        at = jnp.minimum(meta[SLOT_V + h], slots - 1)
        for d in range(directions):
            use = jnp.logical_and(meta[SLOT_V + h] < meta[N_V], place[2 + d] == 1)
            there = jnp.where(use, pick_lane(turned, d * 8 + at), NEG)
            parts.append((there, jnp.where(use, o_back[d, at].astype(jnp.float32), 0.0)))
        attended[:, h * HEAD_DIM : (h + 1) * HEAD_DIM] = merge(parts)[0].astype(jnp.bfloat16)
    width = out.shape[2] // sems.shape[0]
    copies = []
    for j in range(sems.shape[0]):
        at = slice(j * width, (j + 1) * width)
        branch = jnp.dot(attended[...], w_out[:, at], preferred_element_type=jnp.float32)
        branch = (branch * gate[at][None, :]).reshape(tile_tokens, frames, width)
        staged[:, :, at] = (tokens[:, :, at].astype(jnp.float32) + branch).astype(jnp.bfloat16)
        copies.append(pltpu.make_async_copy(staged.at[:, :, at], out.at[:, :, at], sems.at[j]))
        copies[-1].start()
    for copy in copies:
        copy.wait()


def per_device(
    tokens_in, mod_shift, mod_scale, mod_gate, w_qkv, q_gain, k_gain, w_out, windows, frame_lists, frame_valid
):
    frames, _, tile_tokens, feature_dim = tokens_in.shape
    inner = w_out.shape[0]
    heads = windows.shape[0]
    rows = frames * tile_tokens
    slots = heads - 1
    space_size = lax.axis_size("space")
    assert lax.axis_size("tm") == 2
    tile_cols = min(8, space_size // 2)
    tile_rows = space_size // tile_cols
    bf16, f32 = jnp.bfloat16, jnp.float32
    tokens = jnp.transpose(tokens_in[:, 0], (1, 0, 2))

    assert tile_cols % 2 == 0
    spots = range(space_size)
    col = lambda i: i % tile_cols
    pair = [(i, i ^ 1) for i in spots]
    inner_odd = [i for i in spots if col(i) % 2 and col(i) + 1 < tile_cols]
    far = [p for i in inner_odd for p in ((i, i + 1), (i + 1, i))]
    relay = [p for i in inner_odd for p in ((i - 1, i + 1), (i + 2, i))]
    down = [(i, i + tile_cols) for i in spots if i + tile_cols < space_size]
    up = [(j, i) for i, j in down]
    vertical = [down + up] if tile_rows == 2 else [down, up]
    directions = len(vertical)
    swap = [(0, 1), (1, 0)]

    position = lax.axis_index("space")
    tile_row = position // tile_cols
    tile_col = position % tile_cols
    has_partner = (
        [position >= 0] if tile_rows == 2 else [tile_row < tile_rows - 1, tile_row > 0]
    )
    place = jnp.stack(
        [lax.axis_index("tm"), (tile_col > 0) & (tile_col < tile_cols - 1), *has_partner]
    ).astype(jnp.int32)

    meta, q_here, q_send, kv_here = pl.pallas_call(
        functools.partial(project_kernel, heads),
        in_specs=[HBM] * 7,
        out_specs=[SMEM, VMEM, VMEM, VMEM],
        out_shape=[
            jax.ShapeDtypeStruct((META,), jnp.int32),
            jax.ShapeDtypeStruct((heads, rows, HEAD_DIM), bf16),
            jax.ShapeDtypeStruct((slots, rows, HEAD_DIM), bf16),
            jax.ShapeDtypeStruct((heads, 2, rows, HEAD_DIM), bf16),
        ],
        scratch_shapes=[
            pltpu.SMEM((2, heads), jnp.int32),
            pltpu.VMEM(tokens.shape, bf16),
            pltpu.VMEM(mod_shift.shape, f32),
            pltpu.VMEM(mod_scale.shape, f32),
            pltpu.VMEM(q_gain.shape, f32),
            pltpu.VMEM(k_gain.shape, f32),
            pltpu.VMEM((rows, feature_dim), bf16),
            pltpu.VMEM((3, feature_dim, inner), bf16),
            pltpu.SemaphoreType.DMA((6,)),
            pltpu.SemaphoreType.DMA((3,)),
        ],
        compiler_params=params(24),
        name="project",
    )(*[
        pltpu.with_memory_space_constraint(x, pltpu.HBM)
        for x in (windows.T, tokens, mod_shift, mod_scale, w_qkv, q_gain, k_gain)
    ])

    back = [[(j, i) for i, j in pairs] for pairs in vertical]
    lanes = 128
    stat_rows = 256

    def along_row(sent, *operands):
        return row_step(sent, *operands)

    def row_step(sent, kv_here, q_send, q_here, meta):
        k_send, v_send = pl.pallas_call(
            pack_kernel,
            in_specs=[SMEM, VMEM],
            out_specs=[VMEM, VMEM],
            out_shape=[jax.ShapeDtypeStruct((sent, rows, HEAD_DIM), bf16)] * 2,
            compiler_params=params(4),
            name="pack",
        )(meta, kv_here)
        kv_other = lax.ppermute(kv_here, "tm", swap)
        k_pair = lax.ppermute(k_send, "space", pair)
        q_visit = jnp.stack([lax.ppermute(q_send, "space", pairs) for pairs in vertical])
        v_far = lax.ppermute(v_send, "space", far)
        v_pair = lax.ppermute(v_send, "space", pair)
        k_far = lax.ppermute(k_pair, "space", relay)
        k_pair2, v_pair2, k_far2, v_far2 = [
            lax.ppermute(x, "tm", swap) for x in (k_pair, v_pair, k_far, v_far)
        ]
        o_own, lse_own, bias_own, bias_near = pl.pallas_call(
            functools.partial(own_tile_kernel, heads),
            in_specs=[SMEM] * 3 + [VMEM] * 3,
            out_specs=[VMEM] * 4,
            out_shape=[
                jax.ShapeDtypeStruct((heads, rows, HEAD_DIM), f32),
                jax.ShapeDtypeStruct((rows, lanes), f32),
                jax.ShapeDtypeStruct((rows, 2 * rows), f32),
                jax.ShapeDtypeStruct((rows, 4 * rows), f32),
            ],
            compiler_params=params(12),
            cost_estimate=pl.CostEstimate(
                flops=8 * heads * rows * rows * HEAD_DIM, bytes_accessed=6 << 20, transcendentals=2 * heads * rows * rows
            ),
            name="own_tile",
        )(place, frame_lists, frame_valid, q_here, kv_here, kv_other)
        o_near, lse_near, o_visit, lse_visit = pl.pallas_call(
            attend_kernel,
            in_specs=[SMEM] + [VMEM] * 14,
            out_specs=[VMEM] * 4,
            out_shape=[
                jax.ShapeDtypeStruct((sent, rows, HEAD_DIM), f32),
                jax.ShapeDtypeStruct((rows, lanes), f32),
                jax.ShapeDtypeStruct((directions, slots, rows, HEAD_DIM), bf16),
                jax.ShapeDtypeStruct((directions, 8, stat_rows), f32),
            ],
            scratch_shapes=[pltpu.VMEM((stat_rows, lanes), f32)],
            compiler_params=params(24),
            name="attend",
        )(meta, q_here, q_visit, kv_here, kv_other, k_pair, v_pair, k_pair2, v_pair2, k_far, v_far, k_far2, v_far2,
          bias_own, bias_near)
        o_near = jnp.pad(o_near, ((0, slots - sent), (0, 0), (0, 0)))
        return o_own, lse_own, o_near, lse_near, o_visit, lse_visit

    counts = jnp.sum(windows >= 3, axis=0)
    least = min(2, slots)

    def pick(count, branch, *operands):
        return lax.switch(
            count - least, [functools.partial(branch, n) for n in range(least, slots + 1)], *operands
        )

    o_own, lse_own, o_near, lse_near, o_visit, lse_visit = pick(
        counts[1], along_row, kv_here, q_send, q_here, meta
    )

    def between_rows(sent, *operands):
        return return_step(sent, *operands)

    def return_step(sent, o_own, lse_own, o_near, lse_near, o_visit, lse_visit, meta):
        o_back = jnp.stack([lax.ppermute(o_visit[d, :sent], "space", back[d]) for d in range(directions)])
        lse_back = jnp.stack([lax.ppermute(lse_visit[d], "space", back[d]) for d in range(directions)])
        o_row, lse_row = pl.pallas_call(
            functools.partial(row_kernel, heads),
            in_specs=[SMEM] + [VMEM] * 4,
            out_specs=[VMEM] * 2,
            out_shape=[
                jax.ShapeDtypeStruct((heads, rows, HEAD_DIM), f32),
                jax.ShapeDtypeStruct((rows, lanes), f32),
            ],
            compiler_params=params(8),
            cost_estimate=pl.CostEstimate(flops=1 << 22, bytes_accessed=2 << 20, transcendentals=1 << 14),
            name="row_merge",
        )(meta, o_own, lse_own, o_near, lse_near)
        return pl.pallas_call(
            functools.partial(output_kernel, heads),
            in_specs=[SMEM, SMEM] + [VMEM] * 7,
            out_specs=HBM,
            out_shape=pltpu.HBM(tokens.shape, bf16),
            scratch_shapes=[
                pltpu.VMEM((rows, inner), bf16),
                pltpu.VMEM((lanes, stat_rows), f32),
                pltpu.VMEM(tokens.shape, bf16),
                pltpu.SemaphoreType.DMA((3,)),
            ],
            compiler_params=params(16),
            name="output",
        )(meta, place, tokens, mod_gate, w_out, o_row, lse_row, o_back, lse_back)

    mixed = pick(counts[0], between_rows, o_own, lse_own, o_near, lse_near, o_visit, lse_visit, meta)
    return jnp.transpose(mixed, (1, 0, 2))[:, None]


def solution(mesh):
    in_specs = (
        P(("clips", "tm"), "space", None, None),
        P("clips"),
        P("clips"),
        P("clips"),
        P(),
        P(),
        P(),
        P(),
        P(),
        P("clips", None),
        P("clips"),
    )
    out_specs = P(("clips", "tm"), "space", None, None)
    return jax.shard_map(
        per_device, mesh=mesh, in_specs=in_specs, out_specs=out_specs, check_vma=False
    )
```

```python
import functools

import jax
import jax.numpy as jnp
from jax import lax
from jax.experimental import pallas as pl
from jax.experimental.pallas import tpu as pltpu
from jax.sharding import PartitionSpec as P


HEAD_DIM = 128
NEG = -1e30
LOG2E = 1.4426950408889634
N_H, N_V, N_BOTH, SLOT_H, SLOT_V, ORDER_H, ORDER_V = 0, 1, 2, 8, 16, 24, 32
META = 40

VMEM = pl.BlockSpec(memory_space=pltpu.VMEM)
SMEM = pl.BlockSpec(memory_space=pltpu.SMEM)
HBM = pl.BlockSpec(memory_space=pltpu.HBM)


def params(mebibytes):
    return pltpu.CompilerParams(vmem_limit_bytes=mebibytes << 20)


def rank_heads(windows, meta, heads):
    wide = [jnp.where(windows[1, h] >= 3, 1, 0) for h in range(heads)]
    tall = [jnp.where(windows[0, h] >= 3, 1, 0) for h in range(heads)]
    both = [w * t for w, t in zip(wide, tall)]
    meta[N_H], meta[N_V], meta[N_BOTH] = sum(wide), sum(tall), sum(both)
    for classes, slot_at, order_at in (
        ([1 - w for w in wide], SLOT_H, ORDER_H),
        ([2 - t - b for t, b in zip(tall, both)], SLOT_V, ORDER_V),
    ):
        for h in range(heads):
            slot = sum(
                jnp.where((classes[o] < classes[h]) | ((classes[o] == classes[h]) & (o < h)), 1, 0)
                for o in range(heads) if o != h
            )
            meta[slot_at + h] = slot
            meta[order_at + slot] = h


def project_kernel(
    heads, least, windows_at, tokens_at, shift_at, scale_at, w_qkv, q_gain_at, k_gain_at,
    meta, wide_branch, tall_branch, q_here, q_send, kv_here,
    windows, tokens, shift, scale, q_gain, k_gain, modulated, w_buf, small_sems, sems,
):
    tile_tokens, frames, _ = tokens.shape
    inner = heads * HEAD_DIM
    queries, keys, values = 0, 1, 2
    small = [
        pltpu.make_async_copy(there, ref, small_sems.at[i])
        for i, (there, ref) in enumerate((
            (tokens_at, tokens), (shift_at, shift), (scale_at, scale),
            (windows_at, windows), (k_gain_at, k_gain), (q_gain_at, q_gain),
        ))
    ]
    blocks = {
        j: pltpu.make_async_copy(w_qkv.at[:, pl.ds(j * inner, inner)], w_buf.at[j], sems.at[j])
        for j in (keys, values, queries)
    }
    for copy in (*small, blocks[keys]):
        copy.start()
    for copy in small:
        copy.wait()
    rank_heads(windows, meta, heads)
    wide_branch[0] = jnp.clip(meta[N_H] - least, 0, heads - 1 - least)
    tall_branch[0] = jnp.clip(meta[N_V] - least, 0, heads - 1 - least)
    gain_row = 1.0 + scale[...][None, :]
    shift_row = shift[...][None, :]
    step = 4
    for t in range(0, tile_tokens, step):
        if t == tile_tokens // 2 // step * step:
            blocks[values].start()
        floated = tokens[t : t + step].astype(jnp.float32).reshape(step * frames, -1)
        average = jnp.mean(floated, axis=-1, keepdims=True)
        centered = floated - average
        variance = jnp.mean(centered * centered, axis=-1, keepdims=True)
        normed = centered * lax.rsqrt(variance + 1e-06)
        modulated[t * frames : (t + step) * frames] = (normed * gain_row + shift_row).astype(jnp.bfloat16)

    def block(j):
        blocks[j].wait()
        return jnp.dot(modulated[...], w_buf[j], preferred_element_type=jnp.float32)

    def normed_heads(columns, gains):
        squares = jnp.sum(columns * columns, axis=-1, keepdims=True)
        factor = lax.rsqrt(squares * (1.0 / inner) + 1e-06)
        gains_row = gains[...][None, :]
        for h in range(heads):
            at = slice(h * HEAD_DIM, (h + 1) * HEAD_DIM)
            yield h, (columns[:, at] * factor * gains_row[:, at]).astype(jnp.bfloat16)

    columns = block(keys)
    blocks[queries].start()
    for h, part in normed_heads(columns, k_gain):
        kv_here[h, 0] = part
    columns = block(values)
    for h in range(heads):
        kv_here[h, 1] = columns[:, h * HEAD_DIM : (h + 1) * HEAD_DIM].astype(jnp.bfloat16)
    for h, part in normed_heads(block(queries), q_gain):
        q_here[h] = part
    for i in range(q_send.shape[0]):
        q_send[i] = q_here[meta[ORDER_V + i]]


def pack_kernel(meta, kv_here, k_send, v_send):
    for i in range(k_send.shape[0]):
        k_send[i] = kv_here[meta[ORDER_H + i], 0]
        v_send[i] = kv_here[meta[ORDER_H + i], 1]


def softmax_over(query, parts):
    factor = HEAD_DIM**-0.5 * LOG2E
    scores = []
    for pieces, bias in parts:
        keys = jnp.concatenate([key() for key, _ in pieces], axis=0)
        part = lax.dot_general(query, keys, (((1,), (1,)), ((), ())), preferred_element_type=jnp.float32)
        scores.append(part + bias[...])
    peak = functools.reduce(jnp.maximum, [jnp.max(part, axis=1, keepdims=True) for part in scores])
    total, summed = 0.0, 0.0
    for part, (pieces, _) in zip(scores, parts):
        values = jnp.concatenate([value() for _, value in pieces], axis=0)
        weights = jnp.exp2((part - peak) * factor)
        total = total + jnp.sum(weights, axis=1, keepdims=True)
        summed = summed + jnp.dot(weights.astype(jnp.bfloat16), values, preferred_element_type=jnp.float32)
    return summed / total, peak * factor + jnp.log2(total)


def own_pieces(kv_refs, head):
    return [(lambda ref=ref: ref[head, 0], lambda ref=ref: ref[head, 1]) for ref in kv_refs]


def near_pieces(refs, slot):
    return [(lambda k=k: k[slot], lambda v=v: v[slot]) for k, v in refs]


def own_tile_kernel(
    heads, tile_cols, lists, valid, q_here, kv_own, kv_own2, o_own, lse_own, bias_own, bias_near
):
    rows = q_here.shape[1]
    frame_total, listed = lists.shape
    frames = frame_total // 2
    here = lax.axis_index("tm")
    tile_col = lax.rem(lax.axis_index("space"), tile_cols)
    has_far = (tile_col > 0) & (tile_col < tile_cols - 1)
    key_at = lax.broadcasted_iota(jnp.int32, (1, 4 * rows), 1)
    query_at = lax.broadcasted_iota(jnp.int32, (rows, 1), 0)
    part = sum(jnp.where(key_at >= j * rows, 1, 0) for j in range(1, 4))
    frame_slot = (part & 1) * frames + lax.rem(key_at, frames)
    absent = jnp.where((part >= 2) & jnp.logical_not(has_far), NEG, 0.0)
    seen_rows = []
    for f in range(frames):
        row = jnp.full((1, 4 * rows), NEG, jnp.float32)
        for s in range(frame_total):
            frame = (here * frames + s) % frame_total
            query_frame = here * frames + f
            seen = jnp.where(lists[query_frame, 0] == frame, 1, 0)
            for k in range(1, listed):
                seen = seen | jnp.where(lists[query_frame, k] == frame, 1, 0)
            seen = seen & jnp.where(valid[frame] == 1, 1, 0)
            row = jnp.where((frame_slot == s) & (seen == 1), 0.0, row)
        seen_rows.append(row)
    query_frame = lax.rem(query_at, frames)

    def spread(picked):
        full = jnp.broadcast_to(picked[0], (rows, picked[0].shape[1]))
        for f in range(1, frames):
            full = jnp.where(query_frame == f, picked[f], full)
        return full

    bias_own[...] = spread([row[:, : 2 * rows] for row in seen_rows])
    bias_near[...] = spread([jnp.minimum(row, absent) for row in seen_rows])
    lane = lax.broadcasted_iota(jnp.int32, lse_own.shape, 1)
    lse_own[...] = jnp.zeros_like(lse_own)

    @pl.loop(0, heads)
    def _(h):
        out, lse = softmax_over(q_here[h], [(own_pieces((kv_own, kv_own2), h), bias_own)])
        o_own[h] = out
        lse_own[...] = jnp.where(lane == h, lse, lse_own[...])


def attend_kernel(
    meta, q_here, q_visit, kv_own, kv_own2, k_pair, v_pair, k_pair2, v_pair2, k_far, v_far, k_far2, v_far2,
    bias_own, bias_near, o_near, lse_near, o_visit, lse_visit, stats,
):
    directions, _, rows, _ = q_visit.shape
    lane = lax.broadcasted_iota(jnp.int32, (rows, stats.shape[1]), 1)
    stats[...] = jnp.zeros_like(stats)
    sent = k_pair.shape[0]

    def near(slot):
        refs = ((k_pair, v_pair), (k_pair2, v_pair2), (k_far, v_far), (k_far2, v_far2))
        return near_pieces(refs, slot), bias_near

    def own(head):
        return own_pieces((kv_own, kv_own2), head), bias_own

    def keep(lane_at, lse):
        stats[0:rows] = jnp.where(lane == lane_at, lse, stats[0:rows])

    for i in range(sent):
        out, lse = softmax_over(q_here[meta[ORDER_H + i]], [near(i)])
        o_near[i] = out
        keep(i, lse)

    for d in range(directions):
        @pl.loop(0, meta[N_BOTH])
        def _(i, d=d):
            head = meta[ORDER_V + i]
            out, lse = softmax_over(q_visit[d, i], [near(meta[SLOT_H + head]), own(head)])
            o_visit[d, i] = out.astype(o_visit.dtype)
            keep(16 + d * 8 + i, lse)

        @pl.loop(meta[N_BOTH], meta[N_V])
        def _(i, d=d):
            out, lse = softmax_over(q_visit[d, i], [own(meta[ORDER_V + i])])
            o_visit[d, i] = out.astype(o_visit.dtype)
            keep(16 + d * 8 + i, lse)

    lse_near[...] = stats[0:rows]
    turned = jnp.transpose(stats[...])
    for d in range(directions):
        lse_visit[d] = turned[16 + d * 8 : 24 + d * 8]


def merge(parts):
    peak = functools.reduce(jnp.maximum, [lse for lse, _ in parts])
    weights = [jnp.exp2(lse - peak) for lse, _ in parts]
    total = sum(weights[1:], weights[0])
    mixed = sum((w * o for w, (_, o) in zip(weights[1:], parts[1:])), weights[0] * parts[0][1])
    return mixed / total, peak + jnp.log2(total)


def pick_lane(table, at):
    lane = lax.broadcasted_iota(jnp.int32, table.shape, 1)
    return jnp.sum(jnp.where(lane == at, table, 0.0), axis=1, keepdims=True)


def row_kernel(heads, meta, o_own, lse_own, o_near, lse_near, o_row, lse_row):
    lane = lax.broadcasted_iota(jnp.int32, lse_row.shape, 1)
    own, near = lse_own[...], lse_near[...]
    merged = own
    for h in range(heads):
        slot = meta[SLOT_H + h]
        use = slot < meta[N_H]
        at = jnp.minimum(slot, o_near.shape[0] - 1)
        there = jnp.where(use, pick_lane(near, at), NEG)
        result, lse = merge([(own[:, h : h + 1], o_own[h]), (there, jnp.where(use, o_near[at], 0.0))])
        o_row[h] = result
        merged = jnp.where(lane == h, lse, merged)
    lse_row[...] = merged


def output_kernel(
    heads, tile_cols, tile_rows, meta, tokens, gate, w_out, o_row, lse_row, o_back, lse_back,
    out, attended, back, staged, sems,
):
    directions, slots, rows, _ = o_back.shape
    tile_tokens, frames, _ = tokens.shape
    back[...] = jnp.zeros_like(back)
    for d in range(directions):
        back[d * 8 : (d + 1) * 8] = lse_back[d]
    turned = jnp.transpose(back[...])[:rows]
    tile_row = lax.axis_index("space") // tile_cols
    exists = [True] if tile_rows == 2 else [tile_row < tile_rows - 1, tile_row > 0]
    for h in range(heads):
        parts = [(lse_row[:, h : h + 1], o_row[h])]
        at = jnp.minimum(meta[SLOT_V + h], slots - 1)
        for d in range(directions):
            use = jnp.logical_and(meta[SLOT_V + h] < meta[N_V], exists[d])
            there = jnp.where(use, pick_lane(turned, d * 8 + at), NEG)
            parts.append((there, jnp.where(use, o_back[d, at].astype(jnp.float32), 0.0)))
        attended[:, h * HEAD_DIM : (h + 1) * HEAD_DIM] = merge(parts)[0].astype(jnp.bfloat16)
    width = out.shape[2] // sems.shape[0]
    copies = []
    for j in range(sems.shape[0]):
        at = slice(j * width, (j + 1) * width)
        branch = jnp.dot(attended[...], w_out[:, at], preferred_element_type=jnp.float32)
        branch = (branch * gate[at][None, :]).reshape(tile_tokens, frames, width)
        staged[:, :, at] = (tokens[:, :, at].astype(jnp.float32) + branch).astype(jnp.bfloat16)
        copies.append(pltpu.make_async_copy(staged.at[:, :, at], out.at[:, :, at], sems.at[j]))
        copies[-1].start()
    for copy in copies:
        copy.wait()


def branch_on(number, branches, *operands):
    traced = jax.make_jaxpr(lambda *args: lax.switch(args[0], branches, *args[1:]))(number, *operands)
    values = dict(zip(traced.jaxpr.constvars, traced.consts))
    values.update(zip(traced.jaxpr.invars, (number, *operands)))
    (choice,) = [eqn for eqn in traced.jaxpr.eqns if eqn.primitive.name == "cond"]
    outs = choice.primitive.bind(number, *[values[v] for v in choice.invars[1:]], **choice.params)
    values.update(zip(choice.outvars, outs))
    outs = [values[v] for v in traced.jaxpr.outvars]
    return outs[0] if len(outs) == 1 else outs


def per_device(
    tokens_in, mod_shift, mod_scale, mod_gate, w_qkv, q_gain, k_gain, w_out, windows, frame_lists, frame_valid
):
    frames, _, tile_tokens, feature_dim = tokens_in.shape
    inner = w_out.shape[0]
    heads = windows.shape[0]
    rows = frames * tile_tokens
    slots = heads - 1
    space_size = lax.axis_size("space")
    assert lax.axis_size("tm") == 2
    tile_cols = min(8, space_size // 2)
    tile_rows = space_size // tile_cols
    bf16, f32 = jnp.bfloat16, jnp.float32
    tokens = jnp.transpose(tokens_in[:, 0], (1, 0, 2))

    assert tile_cols % 2 == 0
    spots = range(space_size)
    col = lambda i: i % tile_cols
    pair = [(i, i ^ 1) for i in spots]
    inner_odd = [i for i in spots if col(i) % 2 and col(i) + 1 < tile_cols]
    far = [p for i in inner_odd for p in ((i, i + 1), (i + 1, i))]
    relay = [p for i in inner_odd for p in ((i - 1, i + 1), (i + 2, i))]
    down = [(i, i + tile_cols) for i in spots if i + tile_cols < space_size]
    up = [(j, i) for i, j in down]
    vertical = [down + up] if tile_rows == 2 else [down, up]
    directions = len(vertical)
    swap = [(0, 1), (1, 0)]

    least = min(2, slots)
    meta, wide_branch, tall_branch, q_here, q_send, kv_here = pl.pallas_call(
        functools.partial(project_kernel, heads, least),
        in_specs=[HBM] * 7,
        out_specs=[SMEM, SMEM, SMEM, VMEM, VMEM, VMEM],
        out_shape=[
            jax.ShapeDtypeStruct((META,), jnp.int32),
            jax.ShapeDtypeStruct((1,), jnp.int32),
            jax.ShapeDtypeStruct((1,), jnp.int32),
            jax.ShapeDtypeStruct((heads, rows, HEAD_DIM), bf16),
            jax.ShapeDtypeStruct((slots, rows, HEAD_DIM), bf16),
            jax.ShapeDtypeStruct((heads, 2, rows, HEAD_DIM), bf16),
        ],
        scratch_shapes=[
            pltpu.SMEM((2, heads), jnp.int32),
            pltpu.VMEM(tokens.shape, bf16),
            pltpu.VMEM(mod_shift.shape, f32),
            pltpu.VMEM(mod_scale.shape, f32),
            pltpu.VMEM(q_gain.shape, f32),
            pltpu.VMEM(k_gain.shape, f32),
            pltpu.VMEM((rows, feature_dim), bf16),
            pltpu.VMEM((3, feature_dim, inner), bf16),
            pltpu.SemaphoreType.DMA((6,)),
            pltpu.SemaphoreType.DMA((3,)),
        ],
        compiler_params=params(24),
        name="project",
    )(*[
        pltpu.with_memory_space_constraint(x, pltpu.HBM)
        for x in (windows.T, tokens, mod_shift, mod_scale, w_qkv, q_gain, k_gain)
    ])

    back = [[(j, i) for i, j in pairs] for pairs in vertical]
    lanes = 128
    stat_rows = 256

    def along_row(sent, *operands):
        return row_step(sent, *operands)

    def row_step(sent, kv_here, q_send, q_here, meta):
        k_send, v_send = pl.pallas_call(
            pack_kernel,
            in_specs=[SMEM, VMEM],
            out_specs=[VMEM, VMEM],
            out_shape=[jax.ShapeDtypeStruct((sent, rows, HEAD_DIM), bf16)] * 2,
            compiler_params=params(4),
            name="pack",
        )(meta, kv_here)
        kv_other = lax.ppermute(kv_here, "tm", swap)
        k_pair = lax.ppermute(k_send, "space", pair)
        q_visit = jnp.stack([lax.ppermute(q_send, "space", pairs) for pairs in vertical])
        v_far = lax.ppermute(v_send, "space", far)
        v_pair = lax.ppermute(v_send, "space", pair)
        k_far = lax.ppermute(k_pair, "space", relay)
        k_pair2, v_pair2, k_far2, v_far2 = [
            lax.ppermute(x, "tm", swap) for x in (k_pair, v_pair, k_far, v_far)
        ]
        o_own, lse_own, bias_own, bias_near = pl.pallas_call(
            functools.partial(own_tile_kernel, heads, tile_cols),
            in_specs=[SMEM] * 2 + [VMEM] * 3,
            out_specs=[VMEM] * 4,
            out_shape=[
                jax.ShapeDtypeStruct((heads, rows, HEAD_DIM), f32),
                jax.ShapeDtypeStruct((rows, lanes), f32),
                jax.ShapeDtypeStruct((rows, 2 * rows), f32),
                jax.ShapeDtypeStruct((rows, 4 * rows), f32),
            ],
            compiler_params=params(12),
            cost_estimate=pl.CostEstimate(
                flops=8 * heads * rows * rows * HEAD_DIM, bytes_accessed=6 << 20, transcendentals=2 * heads * rows * rows
            ),
            name="own_tile",
        )(frame_lists, frame_valid, q_here, kv_here, kv_other)
        o_near, lse_near, o_visit, lse_visit = pl.pallas_call(
            attend_kernel,
            in_specs=[SMEM] + [VMEM] * 14,
            out_specs=[VMEM] * 4,
            out_shape=[
                jax.ShapeDtypeStruct((sent, rows, HEAD_DIM), f32),
                jax.ShapeDtypeStruct((rows, lanes), f32),
                jax.ShapeDtypeStruct((directions, slots, rows, HEAD_DIM), bf16),
                jax.ShapeDtypeStruct((directions, 8, stat_rows), f32),
            ],
            scratch_shapes=[pltpu.VMEM((stat_rows, lanes), f32)],
            compiler_params=params(24),
            name="attend",
        )(meta, q_here, q_visit, kv_here, kv_other, k_pair, v_pair, k_pair2, v_pair2, k_far, v_far, k_far2, v_far2,
          bias_own, bias_near)
        o_near = jnp.pad(o_near, ((0, slots - sent), (0, 0), (0, 0)))
        return o_own, lse_own, o_near, lse_near, o_visit, lse_visit

    def pick(number, branch, *operands):
        return branch_on(
            number.reshape(()), [functools.partial(branch, n) for n in range(least, slots + 1)], *operands
        )

    o_own, lse_own, o_near, lse_near, o_visit, lse_visit = pick(
        wide_branch, along_row, kv_here, q_send, q_here, meta
    )

    def between_rows(sent, *operands):
        return return_step(sent, *operands)

    def return_step(sent, o_own, lse_own, o_near, lse_near, o_visit, lse_visit, meta):
        o_back = jnp.stack([lax.ppermute(o_visit[d, :sent], "space", back[d]) for d in range(directions)])
        lse_back = jnp.stack([lax.ppermute(lse_visit[d], "space", back[d]) for d in range(directions)])
        o_row, lse_row = pl.pallas_call(
            functools.partial(row_kernel, heads),
            in_specs=[SMEM] + [VMEM] * 4,
            out_specs=[VMEM] * 2,
            out_shape=[
                jax.ShapeDtypeStruct((heads, rows, HEAD_DIM), f32),
                jax.ShapeDtypeStruct((rows, lanes), f32),
            ],
            compiler_params=params(8),
            cost_estimate=pl.CostEstimate(flops=1 << 22, bytes_accessed=2 << 20, transcendentals=1 << 14),
            name="row_merge",
        )(meta, o_own, lse_own, o_near, lse_near)
        return pl.pallas_call(
            functools.partial(output_kernel, heads, tile_cols, tile_rows),
            in_specs=[SMEM] + [VMEM] * 7,
            out_specs=HBM,
            out_shape=pltpu.HBM(tokens.shape, bf16),
            scratch_shapes=[
                pltpu.VMEM((rows, inner), bf16),
                pltpu.VMEM((lanes, stat_rows), f32),
                pltpu.VMEM(tokens.shape, bf16),
                pltpu.SemaphoreType.DMA((3,)),
            ],
            compiler_params=params(16),
            name="output",
        )(meta, tokens, mod_gate, w_out, o_row, lse_row, o_back, lse_back)

    mixed = pick(tall_branch, between_rows, o_own, lse_own, o_near, lse_near, o_visit, lse_visit, meta)
    return jnp.transpose(mixed, (1, 0, 2))[:, None]


def solution(mesh):
    in_specs = (
        P(("clips", "tm"), "space", None, None),
        P("clips"),
        P("clips"),
        P("clips"),
        P(),
        P(),
        P(),
        P(),
        P(),
        P("clips", None),
        P("clips"),
    )
    out_specs = P(("clips", "tm"), "space", None, None)
    return jax.shard_map(
        per_device, mesh=mesh, in_specs=in_specs, out_specs=out_specs, check_vma=False
    )
```

```python
import functools

import jax
import jax.numpy as jnp
from jax import lax
from jax.experimental import pallas as pl
from jax.experimental.pallas import tpu as pltpu
from jax.sharding import PartitionSpec as P


HEAD_DIM = 128
NEG = -1e30
LOG2E = 1.4426950408889634
N_H, N_V, N_BOTH, SLOT_H, SLOT_V, ORDER_H, ORDER_V = 0, 1, 2, 8, 16, 24, 32
META = 40

VMEM = pl.BlockSpec(memory_space=pltpu.VMEM)
SMEM = pl.BlockSpec(memory_space=pltpu.SMEM)
HBM = pl.BlockSpec(memory_space=pltpu.HBM)


def params(mebibytes):
    return pltpu.CompilerParams(vmem_limit_bytes=mebibytes << 20)


def rank_heads(windows, meta, heads):
    wide = [jnp.where(windows[1, h] >= 3, 1, 0) for h in range(heads)]
    tall = [jnp.where(windows[0, h] >= 3, 1, 0) for h in range(heads)]
    both = [w * t for w, t in zip(wide, tall)]
    meta[N_H], meta[N_V], meta[N_BOTH] = sum(wide), sum(tall), sum(both)
    for classes, slot_at, order_at in (
        ([1 - w for w in wide], SLOT_H, ORDER_H),
        ([2 - t - b for t, b in zip(tall, both)], SLOT_V, ORDER_V),
    ):
        for h in range(heads):
            slot = sum(
                jnp.where((classes[o] < classes[h]) | ((classes[o] == classes[h]) & (o < h)), 1, 0)
                for o in range(heads) if o != h
            )
            meta[slot_at + h] = slot
            meta[order_at + slot] = h


def project_kernel(
    heads, least, windows_at, tokens_at, shift_at, scale_at, w_qkv, q_gain_at, k_gain_at,
    meta, wide_branch, tall_branch, q_here, q_send, kv_here,
    windows, tokens, shift, scale, q_gain, k_gain, modulated, w_buf, small_sems, sems,
):
    tile_tokens, frames, _ = tokens.shape
    inner = heads * HEAD_DIM
    queries, keys, values = 0, 1, 2
    small = [
        pltpu.make_async_copy(there, ref, small_sems.at[i])
        for i, (there, ref) in enumerate((
            (tokens_at, tokens), (shift_at, shift), (scale_at, scale),
            (windows_at, windows), (k_gain_at, k_gain), (q_gain_at, q_gain),
        ))
    ]
    blocks = {
        j: pltpu.make_async_copy(w_qkv.at[:, pl.ds(j * inner, inner)], w_buf.at[j], sems.at[j])
        for j in (keys, values, queries)
    }
    for copy in (*small, blocks[keys]):
        copy.start()
    for copy in small:
        copy.wait()
    rank_heads(windows, meta, heads)
    wide_branch[0] = jnp.clip(meta[N_H] - least, 0, heads - 1 - least)
    tall_branch[0] = jnp.clip(meta[N_V] - least, 0, heads - 1 - least)
    gain_row = 1.0 + scale[...][None, :]
    shift_row = shift[...][None, :]
    step = 4
    for t in range(0, tile_tokens, step):
        if t == tile_tokens // 2 // step * step:
            blocks[values].start()
        floated = tokens[t : t + step].astype(jnp.float32).reshape(step * frames, -1)
        average = jnp.mean(floated, axis=-1, keepdims=True)
        centered = floated - average
        variance = jnp.mean(centered * centered, axis=-1, keepdims=True)
        normed = centered * lax.rsqrt(variance + 1e-06)
        modulated[t * frames : (t + step) * frames] = (normed * gain_row + shift_row).astype(jnp.bfloat16)

    def block(j):
        blocks[j].wait()
        return jnp.dot(modulated[...], w_buf[j], preferred_element_type=jnp.float32)

    def normed_heads(columns, gains):
        squares = jnp.sum(columns * columns, axis=-1, keepdims=True)
        factor = lax.rsqrt(squares * (1.0 / inner) + 1e-06)
        gains_row = gains[...][None, :]
        for h in range(heads):
            at = slice(h * HEAD_DIM, (h + 1) * HEAD_DIM)
            yield h, (columns[:, at] * factor * gains_row[:, at]).astype(jnp.bfloat16)

    columns = block(keys)
    blocks[queries].start()
    for h, part in normed_heads(columns, k_gain):
        kv_here[h, 0] = part
    columns = block(values)
    for h in range(heads):
        kv_here[h, 1] = columns[:, h * HEAD_DIM : (h + 1) * HEAD_DIM].astype(jnp.bfloat16)
    for h, part in normed_heads(block(queries), q_gain):
        q_here[h] = part
    for i in range(q_send.shape[0]):
        q_send[i] = q_here[meta[ORDER_V + i]]


def pack_kernel(meta, kv_here, *sends):
    each = sends[0].shape[1]
    for j, send in enumerate(sends):
        for i in range(send.shape[0]):
            send[i] = kv_here[meta[ORDER_H + i], j * each : (j + 1) * each]


def softmax_over(query, parts):
    factor = HEAD_DIM**-0.5 * LOG2E
    scores = []
    for pieces, bias in parts:
        keys = jnp.concatenate([key() for key, _ in pieces], axis=0)
        part = lax.dot_general(query, keys, (((1,), (1,)), ((), ())), preferred_element_type=jnp.float32)
        scores.append(part + bias[...])
    peak = functools.reduce(jnp.maximum, [jnp.max(part, axis=1, keepdims=True) for part in scores])
    total, summed = 0.0, 0.0
    for part, (pieces, _) in zip(scores, parts):
        values = jnp.concatenate([value() for _, value in pieces], axis=0)
        weights = jnp.exp2((part - peak) * factor)
        total = total + jnp.sum(weights, axis=1, keepdims=True)
        summed = summed + jnp.dot(weights.astype(jnp.bfloat16), values, preferred_element_type=jnp.float32)
    return summed / total, peak * factor + jnp.log2(total)


def own_pieces(kv_refs, head):
    return [(lambda ref=ref: ref[head, 0], lambda ref=ref: ref[head, 1]) for ref in kv_refs]


def two_at_a_time(first, last, compute, store):
    @pl.loop(0, lax.shift_right_logical(jnp.int32(last - first + 1), jnp.int32(1)))
    def _(j):
        one = first + 2 * j
        other = jnp.minimum(one + 1, last - 1)
        results = [(i, compute(i)) for i in (one, other)]
        for i, result in results:
            store(i, *result)


def own_tile_kernel(
    heads, tile_cols, lists, valid, q_here, kv_own, kv_own2, o_own, lse_own, bias_own, bias_near
):
    rows = q_here.shape[1]
    frame_total, listed = lists.shape
    frames = frame_total // 2
    here = lax.axis_index("tm")
    tile_col = lax.rem(lax.axis_index("space"), tile_cols)
    has_far = (tile_col > 0) & (tile_col < tile_cols - 1)
    key_at = lax.broadcasted_iota(jnp.int32, (1, 4 * rows), 1)
    query_at = lax.broadcasted_iota(jnp.int32, (rows, 1), 0)
    part = sum(jnp.where(key_at >= j * rows, 1, 0) for j in range(1, 4))
    frame_slot = (part & 1) * frames + lax.rem(key_at, frames)
    absent = jnp.where((part >= 2) & jnp.logical_not(has_far), NEG, 0.0)
    seen_rows = []
    for f in range(frames):
        row = jnp.full((1, 4 * rows), NEG, jnp.float32)
        for s in range(frame_total):
            frame = (here * frames + s) % frame_total
            query_frame = here * frames + f
            seen = jnp.where(lists[query_frame, 0] == frame, 1, 0)
            for k in range(1, listed):
                seen = seen | jnp.where(lists[query_frame, k] == frame, 1, 0)
            seen = seen & jnp.where(valid[frame] == 1, 1, 0)
            row = jnp.where((frame_slot == s) & (seen == 1), 0.0, row)
        seen_rows.append(row)
    query_frame = lax.rem(query_at, frames)

    def spread(picked):
        full = jnp.broadcast_to(picked[0], (rows, picked[0].shape[1]))
        for f in range(1, frames):
            full = jnp.where(query_frame == f, picked[f], full)
        return full

    bias_own[...] = spread([row[:, : 2 * rows] for row in seen_rows])
    bias_near[...] = spread([jnp.minimum(row, absent) for row in seen_rows])
    lane = lax.broadcasted_iota(jnp.int32, lse_own.shape, 1)
    lse_own[...] = jnp.zeros_like(lse_own)

    def compute(h):
        return softmax_over(q_here[h], [(own_pieces((kv_own, kv_own2), h), bias_own)])

    def store(h, out, lse):
        o_own[h] = out
        lse_own[...] = jnp.where(lane == h, lse, lse_own[...])

    two_at_a_time(0, heads, compute, store)


def attend_kernel(parts, meta, q_here, q_visit, kv_own, kv_own2, *refs):
    near_refs, (bias_own, bias_near, o_near, lse_near, o_visit, lse_visit, stats) = refs[:-7], refs[-7:]
    directions, _, rows, _ = q_visit.shape
    lane = lax.broadcasted_iota(jnp.int32, (rows, stats.shape[1]), 1)
    stats[...] = jnp.zeros_like(stats)
    sent = near_refs[0].shape[0]

    def near(slot):
        last = 2 // parts - 1
        pieces = [
            (lambda k=k: k[slot, 0], lambda v=v: v[slot, last])
            for k, v in zip(near_refs[::parts], near_refs[parts - 1 :: parts])
        ]
        return pieces, bias_near

    def own(head):
        return own_pieces((kv_own, kv_own2), head), bias_own

    def keep(lane_at, lse):
        stats[0:rows] = jnp.where(lane == lane_at, lse, stats[0:rows])

    for i in range(sent):
        out, lse = softmax_over(q_here[meta[ORDER_H + i]], [near(i)])
        o_near[i] = out
        keep(i, lse)

    for d in range(directions):
        def store(i, out, lse, d=d):
            o_visit[d, i] = out.astype(o_visit.dtype)
            keep(16 + d * 8 + i, lse)

        def over_row(i, d=d):
            head = meta[ORDER_V + i]
            return softmax_over(q_visit[d, i], [near(meta[SLOT_H + head]), own(head)])

        @pl.loop(0, meta[N_BOTH])
        def _(i, store=store, over_row=over_row):
            store(i, *over_row(i))

        @pl.loop(meta[N_BOTH], meta[N_V])
        def _(i, d=d, store=store):
            store(i, *softmax_over(q_visit[d, i], [own(meta[ORDER_V + i])]))

    lse_near[...] = stats[0:rows]
    turned = jnp.transpose(stats[...])
    for d in range(directions):
        lse_visit[d] = turned[16 + d * 8 : 24 + d * 8]


def merge(parts):
    peak = functools.reduce(jnp.maximum, [lse for lse, _ in parts])
    weights = [jnp.exp2(lse - peak) for lse, _ in parts]
    total = sum(weights[1:], weights[0])
    mixed = sum((w * o for w, (_, o) in zip(weights[1:], parts[1:])), weights[0] * parts[0][1])
    return mixed / total, peak + jnp.log2(total)


def pick_lane(table, at):
    lane = lax.broadcasted_iota(jnp.int32, table.shape, 1)
    return jnp.sum(jnp.where(lane == at, table, 0.0), axis=1, keepdims=True)


def row_kernel(heads, meta, o_own, lse_own, o_near, lse_near, o_row, lse_row, attended):
    lane = lax.broadcasted_iota(jnp.int32, lse_row.shape, 1)
    lse_row[...] = lse_own[...]

    @pl.loop(0, heads)
    def _(h):
        slot = meta[SLOT_H + h]
        use = slot < meta[N_H]
        at = jnp.minimum(slot, o_near.shape[0] - 1)
        there = jnp.where(use, pick_lane(lse_near[...], at), NEG)
        result, lse = merge(
            [(pick_lane(lse_own[...], h), o_own[h]), (there, jnp.where(use, o_near[at], 0.0))]
        )
        o_row[h] = result
        attended[:, pl.ds(pl.multiple_of(h * HEAD_DIM, HEAD_DIM), HEAD_DIM)] = result.astype(jnp.bfloat16)
        lse_row[...] = jnp.where(lane == h, lse, lse_row[...])


def output_kernel(
    tile_cols, tile_rows, meta, tokens, gate, w_out, o_row, lse_row, row_attended, o_back, lse_back,
    out, attended, back, staged, sems,
):
    directions, _, rows, _ = o_back.shape
    tile_tokens, frames, _ = tokens.shape
    for d in range(directions):
        back[d * 8 : (d + 1) * 8] = lse_back[d]
    turned = jnp.transpose(back[...])[:rows]
    tile_row = lax.axis_index("space") // tile_cols
    exists = [True] if tile_rows == 2 else [tile_row < tile_rows - 1, tile_row > 0]
    attended[...] = row_attended[...]

    def compute(i):
        head = meta[ORDER_V + i]
        parts = [(pick_lane(lse_row[...], head), o_row[head])]
        for d in range(directions):
            there = jnp.where(exists[d], pick_lane(turned, d * 8 + i), NEG)
            parts.append((there, jnp.where(exists[d], o_back[d, i].astype(jnp.float32), 0.0)))
        return (merge(parts)[0].astype(jnp.bfloat16),)

    def store(i, mixed):
        at = pl.multiple_of(meta[ORDER_V + i] * HEAD_DIM, HEAD_DIM)
        attended[:, pl.ds(at, HEAD_DIM)] = mixed

    two_at_a_time(0, meta[N_V], compute, store)
    width = out.shape[2] // sems.shape[0]
    copies = []
    for j in range(sems.shape[0]):
        at = slice(j * width, (j + 1) * width)
        branch = jnp.dot(attended[...], w_out[:, at], preferred_element_type=jnp.float32)
        branch = (branch * gate[at][None, :]).reshape(tile_tokens, frames, width)
        staged[:, :, at] = (tokens[:, :, at].astype(jnp.float32) + branch).astype(jnp.bfloat16)
        copies.append(pltpu.make_async_copy(staged.at[:, :, at], out.at[:, :, at], sems.at[j]))
        copies[-1].start()
    for copy in copies:
        copy.wait()


def branch_on(number, branches, *operands):
    traced = jax.make_jaxpr(lambda *args: lax.switch(args[0], branches, *args[1:]))(number, *operands)
    values = dict(zip(traced.jaxpr.constvars, traced.consts))
    values.update(zip(traced.jaxpr.invars, (number, *operands)))
    (choice,) = [eqn for eqn in traced.jaxpr.eqns if eqn.primitive.name == "cond"]
    outs = choice.primitive.bind(number, *[values[v] for v in choice.invars[1:]], **choice.params)
    values.update(zip(choice.outvars, outs))
    outs = [values[v] for v in traced.jaxpr.outvars]
    return outs[0] if len(outs) == 1 else outs


def per_device(
    tokens_in, mod_shift, mod_scale, mod_gate, w_qkv, q_gain, k_gain, w_out, windows, frame_lists, frame_valid
):
    frames, _, tile_tokens, feature_dim = tokens_in.shape
    inner = w_out.shape[0]
    heads = windows.shape[0]
    rows = frames * tile_tokens
    slots = heads - 1
    space_size = lax.axis_size("space")
    assert lax.axis_size("tm") == 2
    tile_cols = min(8, space_size // 2)
    tile_rows = space_size // tile_cols
    bf16, f32 = jnp.bfloat16, jnp.float32
    tokens = jnp.transpose(tokens_in[:, 0], (1, 0, 2))

    assert tile_cols % 2 == 0
    spots = range(space_size)
    col = lambda i: i % tile_cols
    pair = [(i, i ^ 1) for i in spots]
    inner_odd = [i for i in spots if col(i) % 2 and col(i) + 1 < tile_cols]
    far = [p for i in inner_odd for p in ((i, i + 1), (i + 1, i))]
    relay = [p for i in inner_odd for p in ((i - 1, i + 1), (i + 2, i))]
    down = [(i, i + tile_cols) for i in spots if i + tile_cols < space_size]
    up = [(j, i) for i, j in down]
    vertical = [down + up] if tile_rows == 2 else [down, up]
    directions = len(vertical)
    swap = [(0, 1), (1, 0)]

    least, few = min(2, slots), min(3, slots)
    meta, wide_branch, tall_branch, q_here, q_send, kv_here = pl.pallas_call(
        functools.partial(project_kernel, heads, least),
        in_specs=[HBM] * 7,
        out_specs=[SMEM, SMEM, SMEM, VMEM, VMEM, VMEM],
        out_shape=[
            jax.ShapeDtypeStruct((META,), jnp.int32),
            jax.ShapeDtypeStruct((1,), jnp.int32),
            jax.ShapeDtypeStruct((1,), jnp.int32),
            jax.ShapeDtypeStruct((heads, rows, HEAD_DIM), bf16),
            jax.ShapeDtypeStruct((slots, rows, HEAD_DIM), bf16),
            jax.ShapeDtypeStruct((heads, 2, rows, HEAD_DIM), bf16),
        ],
        scratch_shapes=[
            pltpu.SMEM((2, heads), jnp.int32),
            pltpu.VMEM(tokens.shape, bf16),
            pltpu.VMEM(mod_shift.shape, f32),
            pltpu.VMEM(mod_scale.shape, f32),
            pltpu.VMEM(q_gain.shape, f32),
            pltpu.VMEM(k_gain.shape, f32),
            pltpu.VMEM((rows, feature_dim), bf16),
            pltpu.VMEM((3, feature_dim, inner), bf16),
            pltpu.SemaphoreType.DMA((6,)),
            pltpu.SemaphoreType.DMA((3,)),
        ],
        compiler_params=params(24),
        name="project",
    )(*[
        pltpu.with_memory_space_constraint(x, pltpu.HBM)
        for x in (windows.T, tokens, mod_shift, mod_scale, w_qkv, q_gain, k_gain)
    ])

    back = [[(j, i) for i, j in pairs] for pairs in vertical]
    lanes = 128
    stat_rows = 256

    def along_row(sent, *operands):
        return row_step(sent, *operands)

    def row_step(sent, kv_here, q_send, q_here, meta):
        parts = 2 if sent > few else 1
        packed = pl.pallas_call(
            pack_kernel,
            in_specs=[SMEM, VMEM],
            out_specs=[VMEM] * parts,
            out_shape=[jax.ShapeDtypeStruct((sent, 2 // parts, rows, HEAD_DIM), bf16)] * parts,
            compiler_params=params(4),
            name="pack",
        )(meta, kv_here)
        kv_other = lax.ppermute(kv_here, "tm", swap)
        near = [lax.ppermute(packed[0], "space", pair)]
        q_visit = jnp.stack([lax.ppermute(q_send, "space", pairs) for pairs in vertical])
        far_part = lax.ppermute(packed[-1], "space", far)
        if parts == 2:
            near.append(lax.ppermute(packed[1], "space", pair))
            near.append(lax.ppermute(near[0], "space", relay))
        near.append(far_part)
        near = [x for part in near for x in (part, lax.ppermute(part, "tm", swap))]
        if parts == 2:
            near = [near[i] for i in (0, 2, 1, 3, 4, 6, 5, 7)]
        o_own, lse_own, bias_own, bias_near = pl.pallas_call(
            functools.partial(own_tile_kernel, heads, tile_cols),
            in_specs=[SMEM] * 2 + [VMEM] * 3,
            out_specs=[VMEM] * 4,
            out_shape=[
                jax.ShapeDtypeStruct((heads, rows, HEAD_DIM), f32),
                jax.ShapeDtypeStruct((rows, lanes), f32),
                jax.ShapeDtypeStruct((rows, 2 * rows), f32),
                jax.ShapeDtypeStruct((rows, 4 * rows), f32),
            ],
            compiler_params=params(12),
            cost_estimate=pl.CostEstimate(
                flops=8 * heads * rows * rows * HEAD_DIM, bytes_accessed=6 << 20, transcendentals=2 * heads * rows * rows
            ),
            name="own_tile",
        )(frame_lists, frame_valid, q_here, kv_here, kv_other)
        o_near, lse_near, o_visit, lse_visit = pl.pallas_call(
            functools.partial(attend_kernel, parts),
            in_specs=[SMEM] + [VMEM] * (6 + len(near)),
            out_specs=[VMEM] * 4,
            out_shape=[
                jax.ShapeDtypeStruct((slots, rows, HEAD_DIM), f32),
                jax.ShapeDtypeStruct((rows, lanes), f32),
                jax.ShapeDtypeStruct((directions, slots, rows, HEAD_DIM), bf16),
                jax.ShapeDtypeStruct((directions, 8, stat_rows), f32),
            ],
            scratch_shapes=[pltpu.VMEM((stat_rows, lanes), f32)],
            compiler_params=params(24),
            name="attend",
        )(meta, q_here, q_visit, kv_here, kv_other, *near, bias_own, bias_near)
        return o_own, lse_own, o_near, lse_near, o_visit, lse_visit

    o_own, lse_own, o_near, lse_near, o_visit, lse_visit = branch_on(
        wide_branch.reshape(()),
        [functools.partial(along_row, n) for n in range(least, slots + 1)],
        kv_here, q_send, q_here, meta,
    )

    def between_rows(sent, *operands):
        return return_step(sent, *operands)

    def return_step(sent, o_own, lse_own, o_near, lse_near, o_visit, lse_visit, meta):
        o_back = jnp.stack([lax.ppermute(o_visit[d, :sent], "space", back[d]) for d in range(directions)])
        lse_back = jnp.stack([lax.ppermute(lse_visit[d], "space", back[d]) for d in range(directions)])
        row = pl.pallas_call(
            functools.partial(row_kernel, heads),
            in_specs=[SMEM] + [VMEM] * 4,
            out_specs=[VMEM] * 3,
            out_shape=[
                jax.ShapeDtypeStruct((heads, rows, HEAD_DIM), f32),
                jax.ShapeDtypeStruct((rows, lanes), f32),
                jax.ShapeDtypeStruct((rows, inner), bf16),
            ],
            compiler_params=params(8),
            cost_estimate=pl.CostEstimate(flops=1 << 22, bytes_accessed=2 << 20, transcendentals=1 << 14),
            name="row_merge",
        )(meta, o_own, lse_own, o_near, lse_near)
        return pl.pallas_call(
            functools.partial(output_kernel, tile_cols, tile_rows),
            in_specs=[SMEM] + [VMEM] * 8,
            out_specs=HBM,
            out_shape=pltpu.HBM(tokens.shape, bf16),
            scratch_shapes=[
                pltpu.VMEM((rows, inner), bf16),
                pltpu.VMEM((lanes, stat_rows), f32),
                pltpu.VMEM(tokens.shape, bf16),
                pltpu.SemaphoreType.DMA((3,)),
            ],
            compiler_params=params(16),
            name="output",
        )(meta, tokens, mod_gate, w_out, *row, o_back, lse_back)

    mixed = branch_on(
        tall_branch.reshape(()),
        [functools.partial(between_rows, n) for n in range(least, slots + 1)],
        o_own, lse_own, o_near, lse_near, o_visit, lse_visit, meta,
    )
    return jnp.transpose(mixed, (1, 0, 2))[:, None]


def solution(mesh):
    in_specs = (
        P(("clips", "tm"), "space", None, None),
        P("clips"),
        P("clips"),
        P("clips"),
        P(),
        P(),
        P(),
        P(),
        P(),
        P("clips", None),
        P("clips"),
    )
    out_specs = P(("clips", "tm"), "space", None, None)
    return jax.shard_map(
        per_device, mesh=mesh, in_specs=in_specs, out_specs=out_specs, check_vma=False
    )
```

```python
import functools

import jax
import jax.numpy as jnp
from jax import lax
from jax.experimental import pallas as pl
from jax.experimental.pallas import tpu as pltpu
from jax.sharding import PartitionSpec as P


HEAD_DIM = 128
NEG = -1e30
LOG2E = 1.4426950408889634
N_H, N_V, N_BOTH, SLOT_H, SLOT_V, ORDER_H, ORDER_V = 0, 1, 2, 8, 16, 24, 32
META = 40

VMEM = pl.BlockSpec(memory_space=pltpu.VMEM)
SMEM = pl.BlockSpec(memory_space=pltpu.SMEM)
HBM = pl.BlockSpec(memory_space=pltpu.HBM)


def params(mebibytes):
    return pltpu.CompilerParams(vmem_limit_bytes=mebibytes << 20)


def rank_heads(windows, meta, heads):
    wide = [jnp.where(windows[1, h] >= 3, 1, 0) for h in range(heads)]
    tall = [jnp.where(windows[0, h] >= 3, 1, 0) for h in range(heads)]
    both = [w * t for w, t in zip(wide, tall)]
    meta[N_H], meta[N_V], meta[N_BOTH] = sum(wide), sum(tall), sum(both)
    for classes, slot_at, order_at in (
        ([1 - w for w in wide], SLOT_H, ORDER_H),
        ([2 - t - b for t, b in zip(tall, both)], SLOT_V, ORDER_V),
    ):
        for h in range(heads):
            slot = sum(
                jnp.where((classes[o] < classes[h]) | ((classes[o] == classes[h]) & (o < h)), 1, 0)
                for o in range(heads) if o != h
            )
            meta[slot_at + h] = slot
            meta[order_at + slot] = h


def project_kernel(
    heads, least, few, windows_at, tokens_at, shift_at, scale_at, w_qkv, q_gain_at, k_gain_at,
    meta, wide_branch, tall_branch, q_here, q_send, kv_here,
    windows, tokens, shift, scale, q_gain, k_gain, modulated, w_buf, small_sems, sems,
):
    tile_tokens, frames, _ = tokens.shape
    inner = heads * HEAD_DIM
    queries, keys, values = 0, 1, 2
    small = [
        pltpu.make_async_copy(there, ref, small_sems.at[i])
        for i, (there, ref) in enumerate((
            (tokens_at, tokens), (shift_at, shift), (scale_at, scale),
            (windows_at, windows), (k_gain_at, k_gain), (q_gain_at, q_gain),
        ))
    ]
    blocks = {
        j: pltpu.make_async_copy(w_qkv.at[:, pl.ds(j * inner, inner)], w_buf.at[j], sems.at[j])
        for j in (keys, values, queries)
    }
    for copy in (*small, blocks[keys]):
        copy.start()
    for copy in small:
        copy.wait()
    rank_heads(windows, meta, heads)
    wide = jnp.clip(meta[N_H] - least, 0, heads - 1 - least)
    wide_branch[0] = jnp.where((wide == 0) & (meta[N_V] <= few), 0, wide + 1)
    tall_branch[0] = jnp.clip(meta[N_V] - least, 0, heads - 1 - least)
    gain_row = 1.0 + scale[...][None, :]
    shift_row = shift[...][None, :]
    step = 4
    for t in range(0, tile_tokens, step):
        if t == tile_tokens // 2 // step * step:
            blocks[values].start()
        floated = tokens[t : t + step].astype(jnp.float32).reshape(step * frames, -1)
        average = jnp.mean(floated, axis=-1, keepdims=True)
        centered = floated - average
        variance = jnp.mean(centered * centered, axis=-1, keepdims=True)
        normed = centered * lax.rsqrt(variance + 1e-06)
        modulated[t * frames : (t + step) * frames] = (normed * gain_row + shift_row).astype(jnp.bfloat16)

    def block(j):
        blocks[j].wait()
        return jnp.dot(modulated[...], w_buf[j], preferred_element_type=jnp.float32)

    def normed_heads(columns, gains):
        squares = jnp.sum(columns * columns, axis=-1, keepdims=True)
        factor = lax.rsqrt(squares * (1.0 / inner) + 1e-06)
        gains_row = gains[...][None, :]
        for h in range(heads):
            at = slice(h * HEAD_DIM, (h + 1) * HEAD_DIM)
            yield h, (columns[:, at] * factor * gains_row[:, at]).astype(jnp.bfloat16)

    columns = block(keys)
    blocks[queries].start()
    for h, part in normed_heads(columns, k_gain):
        kv_here[h, 0] = part
    columns = block(values)
    for h in range(heads):
        kv_here[h, 1] = columns[:, h * HEAD_DIM : (h + 1) * HEAD_DIM].astype(jnp.bfloat16)
    for h, part in normed_heads(block(queries), q_gain):
        q_here[h] = part
    for i in range(q_send.shape[0]):
        q_send[i] = q_here[meta[ORDER_V + i]]


def pack_kernel(meta, kv_here, *sends):
    each = sends[0].shape[1]
    for j, send in enumerate(sends):
        for i in range(send.shape[0]):
            send[i] = kv_here[meta[ORDER_H + i], j * each : (j + 1) * each]


def softmax_over(query, parts):
    factor = HEAD_DIM**-0.5 * LOG2E
    scores = []
    for pieces, bias in parts:
        keys = jnp.concatenate([key() for key, _ in pieces], axis=0)
        part = lax.dot_general(query, keys, (((1,), (1,)), ((), ())), preferred_element_type=jnp.float32)
        scores.append(part + bias[...])
    peak = functools.reduce(jnp.maximum, [jnp.max(part, axis=1, keepdims=True) for part in scores])
    total, summed = 0.0, 0.0
    for part, (pieces, _) in zip(scores, parts):
        values = jnp.concatenate([value() for _, value in pieces], axis=0)
        weights = jnp.exp2((part - peak) * factor)
        total = total + jnp.sum(weights, axis=1, keepdims=True)
        summed = summed + jnp.dot(weights.astype(jnp.bfloat16), values, preferred_element_type=jnp.float32)
    return summed / total, peak * factor + jnp.log2(total)


def own_pieces(kv_refs, head):
    return [(lambda ref=ref: ref[head, 0], lambda ref=ref: ref[head, 1]) for ref in kv_refs]


def two_at_a_time(first, last, compute, store):
    @pl.loop(0, lax.shift_right_logical(jnp.int32(last - first + 1), jnp.int32(1)))
    def _(j):
        one = first + 2 * j
        other = jnp.minimum(one + 1, last - 1)
        results = [(i, compute(i)) for i in (one, other)]
        for i, result in results:
            store(i, *result)


def own_tile_kernel(
    heads, tile_cols, lists, valid, q_here, kv_own, kv_own2, o_own, lse_own, bias_own, bias_near
):
    rows = q_here.shape[1]
    frame_total, listed = lists.shape
    frames = frame_total // 2
    here = lax.axis_index("tm")
    tile_col = lax.rem(lax.axis_index("space"), tile_cols)
    has_far = (tile_col > 0) & (tile_col < tile_cols - 1)
    key_at = lax.broadcasted_iota(jnp.int32, (1, 4 * rows), 1)
    query_at = lax.broadcasted_iota(jnp.int32, (rows, 1), 0)
    part = sum(jnp.where(key_at >= j * rows, 1, 0) for j in range(1, 4))
    frame_slot = (part & 1) * frames + lax.rem(key_at, frames)
    absent = jnp.where((part >= 2) & jnp.logical_not(has_far), NEG, 0.0)
    seen_rows = []
    for f in range(frames):
        row = jnp.full((1, 4 * rows), NEG, jnp.float32)
        for s in range(frame_total):
            frame = (here * frames + s) % frame_total
            query_frame = here * frames + f
            seen = jnp.where(lists[query_frame, 0] == frame, 1, 0)
            for k in range(1, listed):
                seen = seen | jnp.where(lists[query_frame, k] == frame, 1, 0)
            seen = seen & jnp.where(valid[frame] == 1, 1, 0)
            row = jnp.where((frame_slot == s) & (seen == 1), 0.0, row)
        seen_rows.append(row)
    query_frame = lax.rem(query_at, frames)

    def spread(picked):
        full = jnp.broadcast_to(picked[0], (rows, picked[0].shape[1]))
        for f in range(1, frames):
            full = jnp.where(query_frame == f, picked[f], full)
        return full

    bias_own[...] = spread([row[:, : 2 * rows] for row in seen_rows])
    bias_near[...] = spread([jnp.minimum(row, absent) for row in seen_rows])
    lane = lax.broadcasted_iota(jnp.int32, lse_own.shape, 1)
    lse_own[...] = jnp.zeros_like(lse_own)

    def compute(h):
        return softmax_over(q_here[h], [(own_pieces((kv_own, kv_own2), h), bias_own)])

    def store(h, out, lse):
        o_own[h] = out
        lse_own[...] = jnp.where(lane == h, lse, lse_own[...])

    two_at_a_time(0, heads, compute, store)


def attend_kernel(parts, meta, q_here, q_visit, kv_own, kv_own2, *refs):
    near_refs, (bias_own, bias_near, o_near, lse_near, o_visit, lse_visit, stats) = refs[:-7], refs[-7:]
    directions, _, rows, _ = q_visit.shape
    lane = lax.broadcasted_iota(jnp.int32, (rows, stats.shape[1]), 1)
    stats[...] = jnp.zeros_like(stats)
    sent = near_refs[0].shape[0]

    def near(slot):
        last = 2 // parts - 1
        pieces = [
            (lambda k=k: k[slot, 0], lambda v=v: v[slot, last])
            for k, v in zip(near_refs[::parts], near_refs[parts - 1 :: parts])
        ]
        return pieces, bias_near

    def own(head):
        return own_pieces((kv_own, kv_own2), head), bias_own

    def keep(lane_at, lse):
        stats[0:rows] = jnp.where(lane == lane_at, lse, stats[0:rows])

    for i in range(sent):
        out, lse = softmax_over(q_here[meta[ORDER_H + i]], [near(i)])
        o_near[i] = out
        keep(i, lse)

    for d in range(directions):
        def store(i, out, lse, d=d):
            o_visit[d, i] = out.astype(o_visit.dtype)
            keep(16 + d * 8 + i, lse)

        def over_row(i, d=d):
            head = meta[ORDER_V + i]
            return softmax_over(q_visit[d, i], [near(meta[SLOT_H + head]), own(head)])

        @pl.loop(0, meta[N_BOTH])
        def _(i, store=store, over_row=over_row):
            store(i, *over_row(i))

        @pl.loop(meta[N_BOTH], meta[N_V])
        def _(i, d=d, store=store):
            store(i, *softmax_over(q_visit[d, i], [own(meta[ORDER_V + i])]))

    lse_near[...] = stats[0:rows]
    turned = jnp.transpose(stats[...])
    for d in range(directions):
        lse_visit[d] = turned[16 + d * 8 : 24 + d * 8]


def merge(parts):
    peak = functools.reduce(jnp.maximum, [lse for lse, _ in parts])
    weights = [jnp.exp2(lse - peak) for lse, _ in parts]
    total = sum(weights[1:], weights[0])
    mixed = sum((w * o for w, (_, o) in zip(weights[1:], parts[1:])), weights[0] * parts[0][1])
    return mixed / total, peak + jnp.log2(total)


def pick_lane(table, at):
    lane = lax.broadcasted_iota(jnp.int32, table.shape, 1)
    return jnp.sum(jnp.where(lane == at, table, 0.0), axis=1, keepdims=True)


def row_kernel(heads, meta, o_own, lse_own, o_near, lse_near, o_row, lse_row, attended):
    lane = lax.broadcasted_iota(jnp.int32, lse_row.shape, 1)
    lse_row[...] = lse_own[...]

    @pl.loop(0, heads)
    def _(h):
        slot = meta[SLOT_H + h]
        use = slot < meta[N_H]
        at = jnp.minimum(slot, o_near.shape[0] - 1)
        there = jnp.where(use, pick_lane(lse_near[...], at), NEG)
        result, lse = merge(
            [(pick_lane(lse_own[...], h), o_own[h]), (there, jnp.where(use, o_near[at], 0.0))]
        )
        o_row[h] = result
        attended[:, pl.ds(pl.multiple_of(h * HEAD_DIM, HEAD_DIM), HEAD_DIM)] = result.astype(jnp.bfloat16)
        lse_row[...] = jnp.where(lane == h, lse, lse_row[...])


def output_kernel(
    tile_cols, tile_rows, meta, tokens, gate, w_out, o_row, lse_row, row_attended, o_back, lse_back,
    out, attended, back, staged, sems,
):
    directions, _, rows, _ = o_back.shape
    tile_tokens, frames, _ = tokens.shape
    for d in range(directions):
        back[d * 8 : (d + 1) * 8] = lse_back[d]
    turned = jnp.transpose(back[...])[:rows]
    tile_row = lax.axis_index("space") // tile_cols
    exists = [True] if tile_rows == 2 else [tile_row < tile_rows - 1, tile_row > 0]
    attended[...] = row_attended[...]

    def compute(i):
        head = meta[ORDER_V + i]
        parts = [(pick_lane(lse_row[...], head), o_row[head])]
        for d in range(directions):
            there = jnp.where(exists[d], pick_lane(turned, d * 8 + i), NEG)
            parts.append((there, jnp.where(exists[d], o_back[d, i].astype(jnp.float32), 0.0)))
        return (merge(parts)[0].astype(jnp.bfloat16),)

    def store(i, mixed):
        at = pl.multiple_of(meta[ORDER_V + i] * HEAD_DIM, HEAD_DIM)
        attended[:, pl.ds(at, HEAD_DIM)] = mixed

    two_at_a_time(0, meta[N_V], compute, store)
    width = out.shape[2] // sems.shape[0]
    copies = []
    for j in range(sems.shape[0]):
        at = slice(j * width, (j + 1) * width)
        branch = jnp.dot(attended[...], w_out[:, at], preferred_element_type=jnp.float32)
        branch = (branch * gate[at][None, :]).reshape(tile_tokens, frames, width)
        staged[:, :, at] = (tokens[:, :, at].astype(jnp.float32) + branch).astype(jnp.bfloat16)
        copies.append(pltpu.make_async_copy(staged.at[:, :, at], out.at[:, :, at], sems.at[j]))
        copies[-1].start()
    for copy in copies:
        copy.wait()


def branch_on(number, branches, *operands):
    traced = jax.make_jaxpr(lambda *args: lax.switch(args[0], branches, *args[1:]))(number, *operands)
    values = dict(zip(traced.jaxpr.constvars, traced.consts))
    values.update(zip(traced.jaxpr.invars, (number, *operands)))
    (choice,) = [eqn for eqn in traced.jaxpr.eqns if eqn.primitive.name == "cond"]
    outs = choice.primitive.bind(number, *[values[v] for v in choice.invars[1:]], **choice.params)
    values.update(zip(choice.outvars, outs))
    outs = [values[v] for v in traced.jaxpr.outvars]
    return outs[0] if len(outs) == 1 else outs


def per_device(
    tokens_in, mod_shift, mod_scale, mod_gate, w_qkv, q_gain, k_gain, w_out, windows, frame_lists, frame_valid
):
    frames, _, tile_tokens, feature_dim = tokens_in.shape
    inner = w_out.shape[0]
    heads = windows.shape[0]
    rows = frames * tile_tokens
    slots = heads - 1
    space_size = lax.axis_size("space")
    assert lax.axis_size("tm") == 2
    tile_cols = min(8, space_size // 2)
    tile_rows = space_size // tile_cols
    bf16, f32 = jnp.bfloat16, jnp.float32
    tokens = jnp.transpose(tokens_in[:, 0], (1, 0, 2))

    assert tile_cols % 2 == 0
    spots = range(space_size)
    col = lambda i: i % tile_cols
    pair = [(i, i ^ 1) for i in spots]
    inner_odd = [i for i in spots if col(i) % 2 and col(i) + 1 < tile_cols]
    far = [p for i in inner_odd for p in ((i, i + 1), (i + 1, i))]
    relay = [p for i in inner_odd for p in ((i - 1, i + 1), (i + 2, i))]
    down = [(i, i + tile_cols) for i in spots if i + tile_cols < space_size]
    up = [(j, i) for i, j in down]
    vertical = [down + up] if tile_rows == 2 else [down, up]
    directions = len(vertical)
    swap = [(0, 1), (1, 0)]

    least, few = min(2, slots), min(3, slots)
    meta, wide_branch, tall_branch, q_here, q_send, kv_here = pl.pallas_call(
        functools.partial(project_kernel, heads, least, few),
        in_specs=[HBM] * 7,
        out_specs=[SMEM, SMEM, SMEM, VMEM, VMEM, VMEM],
        out_shape=[
            jax.ShapeDtypeStruct((META,), jnp.int32),
            jax.ShapeDtypeStruct((1,), jnp.int32),
            jax.ShapeDtypeStruct((1,), jnp.int32),
            jax.ShapeDtypeStruct((heads, rows, HEAD_DIM), bf16),
            jax.ShapeDtypeStruct((slots, rows, HEAD_DIM), bf16),
            jax.ShapeDtypeStruct((heads, 2, rows, HEAD_DIM), bf16),
        ],
        scratch_shapes=[
            pltpu.SMEM((2, heads), jnp.int32),
            pltpu.VMEM(tokens.shape, bf16),
            pltpu.VMEM(mod_shift.shape, f32),
            pltpu.VMEM(mod_scale.shape, f32),
            pltpu.VMEM(q_gain.shape, f32),
            pltpu.VMEM(k_gain.shape, f32),
            pltpu.VMEM((rows, feature_dim), bf16),
            pltpu.VMEM((3, feature_dim, inner), bf16),
            pltpu.SemaphoreType.DMA((6,)),
            pltpu.SemaphoreType.DMA((3,)),
        ],
        compiler_params=params(24),
        name="project",
    )(*[
        pltpu.with_memory_space_constraint(x, pltpu.HBM)
        for x in (windows.T, tokens, mod_shift, mod_scale, w_qkv, q_gain, k_gain)
    ])

    back = [[(j, i) for i, j in pairs] for pairs in vertical]
    lanes = 128
    stat_rows = 256

    def along_row(sent, asked, *operands):
        return row_step(sent, asked, *operands)

    def row_step(sent, asked, kv_here, q_send, q_here, meta):
        parts = 2 if sent > few else 1
        packed = pl.pallas_call(
            pack_kernel,
            in_specs=[SMEM, VMEM],
            out_specs=[VMEM] * parts,
            out_shape=[jax.ShapeDtypeStruct((sent, 2 // parts, rows, HEAD_DIM), bf16)] * parts,
            compiler_params=params(4),
            name="pack",
        )(meta, kv_here)
        kv_other = lax.ppermute(kv_here, "tm", swap)
        near = [lax.ppermute(packed[0], "space", pair)]
        q_visit = jnp.stack([lax.ppermute(q_send[:asked], "space", pairs) for pairs in vertical])
        far_part = lax.ppermute(packed[-1], "space", far)
        if parts == 2:
            near.append(lax.ppermute(packed[1], "space", pair))
            near.append(lax.ppermute(near[0], "space", relay))
        near.append(far_part)
        near = [x for part in near for x in (part, lax.ppermute(part, "tm", swap))]
        if parts == 2:
            near = [near[i] for i in (0, 2, 1, 3, 4, 6, 5, 7)]
        o_own, lse_own, bias_own, bias_near = pl.pallas_call(
            functools.partial(own_tile_kernel, heads, tile_cols),
            in_specs=[SMEM] * 2 + [VMEM] * 3,
            out_specs=[VMEM] * 4,
            out_shape=[
                jax.ShapeDtypeStruct((heads, rows, HEAD_DIM), f32),
                jax.ShapeDtypeStruct((rows, lanes), f32),
                jax.ShapeDtypeStruct((rows, 2 * rows), f32),
                jax.ShapeDtypeStruct((rows, 4 * rows), f32),
            ],
            compiler_params=params(12),
            cost_estimate=pl.CostEstimate(
                flops=8 * heads * rows * rows * HEAD_DIM, bytes_accessed=6 << 20, transcendentals=2 * heads * rows * rows
            ),
            name="own_tile",
        )(frame_lists, frame_valid, q_here, kv_here, kv_other)
        o_near, lse_near, o_visit, lse_visit = pl.pallas_call(
            functools.partial(attend_kernel, parts),
            in_specs=[SMEM] + [VMEM] * (6 + len(near)),
            out_specs=[VMEM] * 4,
            out_shape=[
                jax.ShapeDtypeStruct((slots, rows, HEAD_DIM), f32),
                jax.ShapeDtypeStruct((rows, lanes), f32),
                jax.ShapeDtypeStruct((directions, slots, rows, HEAD_DIM), bf16),
                jax.ShapeDtypeStruct((directions, 8, stat_rows), f32),
            ],
            scratch_shapes=[pltpu.VMEM((stat_rows, lanes), f32)],
            compiler_params=params(24),
            name="attend",
        )(meta, q_here, q_visit, kv_here, kv_other, *near, bias_own, bias_near)
        return o_own, lse_own, o_near, lse_near, o_visit, lse_visit

    ways = [(n, asked) for n in range(least, slots + 1) for asked in ((few, slots) if n == least else (slots,))]
    o_own, lse_own, o_near, lse_near, o_visit, lse_visit = branch_on(
        wide_branch.reshape(()),
        [functools.partial(along_row, *way) for way in ways],
        kv_here, q_send, q_here, meta,
    )

    def between_rows(sent, *operands):
        return return_step(sent, *operands)

    def return_step(sent, o_own, lse_own, o_near, lse_near, o_visit, lse_visit, meta):
        o_back = jnp.stack([lax.ppermute(o_visit[d, :sent], "space", back[d]) for d in range(directions)])
        lse_back = jnp.stack([lax.ppermute(lse_visit[d], "space", back[d]) for d in range(directions)])
        row = pl.pallas_call(
            functools.partial(row_kernel, heads),
            in_specs=[SMEM] + [VMEM] * 4,
            out_specs=[VMEM] * 3,
            out_shape=[
                jax.ShapeDtypeStruct((heads, rows, HEAD_DIM), f32),
                jax.ShapeDtypeStruct((rows, lanes), f32),
                jax.ShapeDtypeStruct((rows, inner), bf16),
            ],
            compiler_params=params(8),
            cost_estimate=pl.CostEstimate(flops=1 << 22, bytes_accessed=2 << 20, transcendentals=1 << 14),
            name="row_merge",
        )(meta, o_own, lse_own, o_near, lse_near)
        return pl.pallas_call(
            functools.partial(output_kernel, tile_cols, tile_rows),
            in_specs=[SMEM] + [VMEM] * 8,
            out_specs=HBM,
            out_shape=pltpu.HBM(tokens.shape, bf16),
            scratch_shapes=[
                pltpu.VMEM((rows, inner), bf16),
                pltpu.VMEM((lanes, stat_rows), f32),
                pltpu.VMEM(tokens.shape, bf16),
                pltpu.SemaphoreType.DMA((3,)),
            ],
            compiler_params=params(16),
            name="output",
        )(meta, tokens, mod_gate, w_out, *row, o_back, lse_back)

    mixed = branch_on(
        tall_branch.reshape(()),
        [functools.partial(between_rows, n) for n in range(least, slots + 1)],
        o_own, lse_own, o_near, lse_near, o_visit, lse_visit, meta,
    )
    return jnp.transpose(mixed, (1, 0, 2))[:, None]


def solution(mesh):
    in_specs = (
        P(("clips", "tm"), "space", None, None),
        P("clips"),
        P("clips"),
        P("clips"),
        P(),
        P(),
        P(),
        P(),
        P(),
        P("clips", None),
        P("clips"),
    )
    out_specs = P(("clips", "tm"), "space", None, None)
    return jax.shard_map(
        per_device, mesh=mesh, in_specs=in_specs, out_specs=out_specs, check_vma=False
    )
```

```python
import functools

import jax
import jax.numpy as jnp
from jax import lax
from jax.experimental import pallas as pl
from jax.experimental.pallas import tpu as pltpu
from jax.sharding import PartitionSpec as P


HEAD_DIM = 128
NEG = -1e30
LOG2E = 1.4426950408889634
N_H, N_V, N_BOTH, SLOT_H, SLOT_V, ORDER_H, ORDER_V = 0, 1, 2, 8, 16, 24, 32
META = 40

VMEM = pl.BlockSpec(memory_space=pltpu.VMEM)
SMEM = pl.BlockSpec(memory_space=pltpu.SMEM)
HBM = pl.BlockSpec(memory_space=pltpu.HBM)


def params(mebibytes):
    return pltpu.CompilerParams(vmem_limit_bytes=mebibytes << 20)


def rank_heads(windows, meta, heads):
    wide = [jnp.where(windows[1, h] >= 3, 1, 0) for h in range(heads)]
    tall = [jnp.where(windows[0, h] >= 3, 1, 0) for h in range(heads)]
    both = [w * t for w, t in zip(wide, tall)]
    meta[N_H], meta[N_V], meta[N_BOTH] = sum(wide), sum(tall), sum(both)
    for classes, slot_at, order_at in (
        ([1 - w for w in wide], SLOT_H, ORDER_H),
        ([2 - t - b for t, b in zip(tall, both)], SLOT_V, ORDER_V),
    ):
        for h in range(heads):
            slot = sum(
                jnp.where((classes[o] < classes[h]) | ((classes[o] == classes[h]) & (o < h)), 1, 0)
                for o in range(heads) if o != h
            )
            meta[slot_at + h] = slot
            meta[order_at + slot] = h


def project_kernel(
    heads, least, few, windows_at, tokens_at, shift_at, scale_at, w_qkv, q_gain_at, k_gain_at,
    meta, wide_branch, tall_branch, q_here, q_send, kv_here, kv_send,
    windows, tokens, shift, scale, q_gain, k_gain, modulated, w_buf, small_sems, sems,
):
    tile_tokens, frames, _ = tokens.shape
    inner = heads * HEAD_DIM
    queries, keys, values = 0, 1, 2
    small = [
        pltpu.make_async_copy(there, ref, small_sems.at[i])
        for i, (there, ref) in enumerate((
            (tokens_at, tokens), (shift_at, shift), (scale_at, scale),
            (windows_at, windows), (k_gain_at, k_gain), (q_gain_at, q_gain),
        ))
    ]
    blocks = {
        j: pltpu.make_async_copy(w_qkv.at[:, pl.ds(j * inner, inner)], w_buf.at[j], sems.at[j])
        for j in (keys, values, queries)
    }
    for copy in (*small, blocks[keys]):
        copy.start()
    for copy in small:
        copy.wait()
    rank_heads(windows, meta, heads)
    wide = jnp.clip(meta[N_H] - least, 0, heads - 1 - least)
    wide_branch[0] = jnp.where((wide == 0) & (meta[N_V] <= few), 0, wide + 1)
    tall_branch[0] = jnp.clip(meta[N_V] - least, 0, heads - 1 - least)
    gain_row = 1.0 + scale[...][None, :]
    shift_row = shift[...][None, :]
    step = 4
    for t in range(0, tile_tokens, step):
        if t == tile_tokens // 2 // step * step:
            blocks[values].start()
        floated = tokens[t : t + step].astype(jnp.float32).reshape(step * frames, -1)
        average = jnp.mean(floated, axis=-1, keepdims=True)
        centered = floated - average
        variance = jnp.mean(centered * centered, axis=-1, keepdims=True)
        normed = centered * lax.rsqrt(variance + 1e-06)
        modulated[t * frames : (t + step) * frames] = (normed * gain_row + shift_row).astype(jnp.bfloat16)

    def block(j):
        blocks[j].wait()
        return jnp.dot(modulated[...], w_buf[j], preferred_element_type=jnp.float32)

    def normed_heads(columns, gains):
        squares = jnp.sum(columns * columns, axis=-1, keepdims=True)
        factor = lax.rsqrt(squares * (1.0 / inner) + 1e-06)
        gains_row = gains[...][None, :]
        for h in range(heads):
            at = slice(h * HEAD_DIM, (h + 1) * HEAD_DIM)
            yield h, (columns[:, at] * factor * gains_row[:, at]).astype(jnp.bfloat16)

    columns = block(keys)
    blocks[queries].start()
    for h, part in normed_heads(columns, k_gain):
        kv_here[h, 0] = part
    columns = block(values)
    for h in range(heads):
        kv_here[h, 1] = columns[:, h * HEAD_DIM : (h + 1) * HEAD_DIM].astype(jnp.bfloat16)
    for h, part in normed_heads(block(queries), q_gain):
        q_here[h] = part
    for i in range(kv_send.shape[0]):
        kv_send[i] = kv_here[meta[ORDER_H + i]]
    for i in range(q_send.shape[0]):
        q_send[i] = q_here[meta[ORDER_V + i]]


def softmax_over(query, parts):
    factor = HEAD_DIM**-0.5 * LOG2E
    scores = []
    for pieces, bias in parts:
        keys = jnp.concatenate([key() for key, _ in pieces], axis=0)
        part = lax.dot_general(query, keys, (((1,), (1,)), ((), ())), preferred_element_type=jnp.float32)
        scores.append(part + bias[...])
    peak = functools.reduce(jnp.maximum, [jnp.max(part, axis=1, keepdims=True) for part in scores])
    total, summed = 0.0, 0.0
    for part, (pieces, _) in zip(scores, parts):
        values = jnp.concatenate([value() for _, value in pieces], axis=0)
        weights = jnp.exp2((part - peak) * factor)
        total = total + jnp.sum(weights, axis=1, keepdims=True)
        summed = summed + jnp.dot(weights.astype(jnp.bfloat16), values, preferred_element_type=jnp.float32)
    return summed / total, peak * factor + jnp.log2(total)


def own_pieces(kv_refs, head):
    return [(lambda ref=ref: ref[head, 0], lambda ref=ref: ref[head, 1]) for ref in kv_refs]


def two_at_a_time(first, last, compute, store):
    @pl.loop(0, lax.shift_right_logical(jnp.int32(last - first + 1), jnp.int32(1)))
    def _(j):
        one = first + 2 * j
        other = jnp.minimum(one + 1, last - 1)
        results = [(i, compute(i)) for i in (one, other)]
        for i, result in results:
            store(i, *result)


def own_tile_kernel(
    heads, tile_cols, lists, valid, q_here, kv_own, kv_own2, o_own, lse_own, bias_own, bias_near
):
    rows = q_here.shape[1]
    frame_total, listed = lists.shape
    frames = frame_total // 2
    here = lax.axis_index("tm")
    tile_col = lax.rem(lax.axis_index("space"), tile_cols)
    has_far = (tile_col > 0) & (tile_col < tile_cols - 1)
    key_at = lax.broadcasted_iota(jnp.int32, (1, 4 * rows), 1)
    query_at = lax.broadcasted_iota(jnp.int32, (rows, 1), 0)
    part = sum(jnp.where(key_at >= j * rows, 1, 0) for j in range(1, 4))
    frame_slot = (part & 1) * frames + lax.rem(key_at, frames)
    absent = jnp.where((part >= 2) & jnp.logical_not(has_far), NEG, 0.0)
    seen_rows = []
    for f in range(frames):
        row = jnp.full((1, 4 * rows), NEG, jnp.float32)
        for s in range(frame_total):
            frame = (here * frames + s) % frame_total
            query_frame = here * frames + f
            seen = jnp.where(lists[query_frame, 0] == frame, 1, 0)
            for k in range(1, listed):
                seen = seen | jnp.where(lists[query_frame, k] == frame, 1, 0)
            seen = seen & jnp.where(valid[frame] == 1, 1, 0)
            row = jnp.where((frame_slot == s) & (seen == 1), 0.0, row)
        seen_rows.append(row)
    query_frame = lax.rem(query_at, frames)

    def spread(picked):
        full = jnp.broadcast_to(picked[0], (rows, picked[0].shape[1]))
        for f in range(1, frames):
            full = jnp.where(query_frame == f, picked[f], full)
        return full

    bias_own[...] = spread([row[:, : 2 * rows] for row in seen_rows])
    bias_near[...] = spread([jnp.minimum(row, absent) for row in seen_rows])
    lane = lax.broadcasted_iota(jnp.int32, lse_own.shape, 1)
    lse_own[...] = jnp.zeros_like(lse_own)

    def compute(h):
        return softmax_over(q_here[h], [(own_pieces((kv_own, kv_own2), h), bias_own)])

    def store(h, out, lse):
        o_own[h] = out
        lse_own[...] = jnp.where(lane == h, lse, lse_own[...])

    two_at_a_time(0, heads, compute, store)


def attend_kernel(parts, meta, q_here, q_visit, kv_own, kv_own2, *refs):
    near_refs, (bias_own, bias_near, o_near, lse_near, o_visit, lse_visit, stats) = refs[:-7], refs[-7:]
    directions, _, rows, _ = q_visit.shape
    lane = lax.broadcasted_iota(jnp.int32, (rows, stats.shape[1]), 1)
    stats[...] = jnp.zeros_like(stats)
    sent = near_refs[0].shape[0]

    def near(slot):
        last = 2 // parts - 1
        pieces = [
            (lambda k=k: k[slot, 0], lambda v=v: v[slot, last])
            for k, v in zip(near_refs[::parts], near_refs[parts - 1 :: parts])
        ]
        return pieces, bias_near

    def own(head):
        return own_pieces((kv_own, kv_own2), head), bias_own

    def keep(lane_at, lse):
        stats[0:rows] = jnp.where(lane == lane_at, lse, stats[0:rows])

    for i in range(sent):
        out, lse = softmax_over(q_here[meta[ORDER_H + i]], [near(i)])
        o_near[i] = out
        keep(i, lse)

    for d in range(directions):
        def store(i, out, lse, d=d):
            o_visit[d, i] = out.astype(o_visit.dtype)
            keep(16 + d * 8 + i, lse)

        def over_row(i, d=d):
            head = meta[ORDER_V + i]
            return softmax_over(q_visit[d, i], [near(meta[SLOT_H + head]), own(head)])

        @pl.loop(0, meta[N_BOTH])
        def _(i, store=store, over_row=over_row):
            store(i, *over_row(i))

        @pl.loop(meta[N_BOTH], meta[N_V])
        def _(i, d=d, store=store):
            store(i, *softmax_over(q_visit[d, i], [own(meta[ORDER_V + i])]))

    lse_near[...] = stats[0:rows]
    turned = jnp.transpose(stats[...])
    for d in range(directions):
        lse_visit[d] = turned[16 + d * 8 : 24 + d * 8]


def merge(parts):
    peak = functools.reduce(jnp.maximum, [lse for lse, _ in parts])
    weights = [jnp.exp2(lse - peak) for lse, _ in parts]
    total = sum(weights[1:], weights[0])
    mixed = sum((w * o for w, (_, o) in zip(weights[1:], parts[1:])), weights[0] * parts[0][1])
    return mixed / total, peak + jnp.log2(total)


def pick_lane(table, at):
    lane = lax.broadcasted_iota(jnp.int32, table.shape, 1)
    return jnp.sum(jnp.where(lane == at, table, 0.0), axis=1, keepdims=True)


def row_kernel(heads, meta, o_own, lse_own, o_near, lse_near, o_row, lse_row, attended):
    lane = lax.broadcasted_iota(jnp.int32, lse_row.shape, 1)
    lse_row[...] = lse_own[...]

    @pl.loop(0, heads)
    def _(h):
        slot = meta[SLOT_H + h]
        use = slot < meta[N_H]
        at = jnp.minimum(slot, o_near.shape[0] - 1)
        there = jnp.where(use, pick_lane(lse_near[...], at), NEG)
        result, lse = merge(
            [(pick_lane(lse_own[...], h), o_own[h]), (there, jnp.where(use, o_near[at], 0.0))]
        )
        o_row[h] = result
        attended[:, pl.ds(pl.multiple_of(h * HEAD_DIM, HEAD_DIM), HEAD_DIM)] = result.astype(jnp.bfloat16)
        lse_row[...] = jnp.where(lane == h, lse, lse_row[...])


def output_kernel(
    tile_cols, tile_rows, meta, tokens, gate, w_out, o_row, lse_row, row_attended, o_back, lse_back,
    out, attended, back, staged, sems,
):
    directions, _, rows, _ = o_back.shape
    tile_tokens, frames, _ = tokens.shape
    for d in range(directions):
        back[d * 8 : (d + 1) * 8] = lse_back[d]
    turned = jnp.transpose(back[...])[:rows]
    tile_row = lax.axis_index("space") // tile_cols
    exists = [True] if tile_rows == 2 else [tile_row < tile_rows - 1, tile_row > 0]
    attended[...] = row_attended[...]

    def compute(i):
        head = meta[ORDER_V + i]
        parts = [(pick_lane(lse_row[...], head), o_row[head])]
        for d in range(directions):
            there = jnp.where(exists[d], pick_lane(turned, d * 8 + i), NEG)
            parts.append((there, jnp.where(exists[d], o_back[d, i].astype(jnp.float32), 0.0)))
        return (merge(parts)[0].astype(jnp.bfloat16),)

    def store(i, mixed):
        at = pl.multiple_of(meta[ORDER_V + i] * HEAD_DIM, HEAD_DIM)
        attended[:, pl.ds(at, HEAD_DIM)] = mixed

    two_at_a_time(0, meta[N_V], compute, store)
    width = out.shape[2] // sems.shape[0]
    copies = []
    for j in range(sems.shape[0]):
        at = slice(j * width, (j + 1) * width)
        branch = jnp.dot(attended[...], w_out[:, at], preferred_element_type=jnp.float32)
        branch = (branch * gate[at][None, :]).reshape(tile_tokens, frames, width)
        staged[:, :, at] = (tokens[:, :, at].astype(jnp.float32) + branch).astype(jnp.bfloat16)
        copies.append(pltpu.make_async_copy(staged.at[:, :, at], out.at[:, :, at], sems.at[j]))
        copies[-1].start()
    for copy in copies:
        copy.wait()


def branch_on(number, branches, *operands):
    traced = jax.make_jaxpr(lambda *args: lax.switch(args[0], branches, *args[1:]))(number, *operands)
    values = dict(zip(traced.jaxpr.constvars, traced.consts))
    values.update(zip(traced.jaxpr.invars, (number, *operands)))
    (choice,) = [eqn for eqn in traced.jaxpr.eqns if eqn.primitive.name == "cond"]
    outs = choice.primitive.bind(number, *[values[v] for v in choice.invars[1:]], **choice.params)
    values.update(zip(choice.outvars, outs))
    outs = [values[v] for v in traced.jaxpr.outvars]
    return outs[0] if len(outs) == 1 else outs


def per_device(
    tokens_in, mod_shift, mod_scale, mod_gate, w_qkv, q_gain, k_gain, w_out, windows, frame_lists, frame_valid
):
    frames, _, tile_tokens, feature_dim = tokens_in.shape
    inner = w_out.shape[0]
    heads = windows.shape[0]
    rows = frames * tile_tokens
    slots = heads - 1
    space_size = lax.axis_size("space")
    assert lax.axis_size("tm") == 2
    tile_cols = min(8, space_size // 2)
    tile_rows = space_size // tile_cols
    bf16, f32 = jnp.bfloat16, jnp.float32
    tokens = jnp.transpose(tokens_in[:, 0], (1, 0, 2))

    assert tile_cols % 2 == 0
    spots = range(space_size)
    col = lambda i: i % tile_cols
    pair = [(i, i ^ 1) for i in spots]
    inner_odd = [i for i in spots if col(i) % 2 and col(i) + 1 < tile_cols]
    far = [p for i in inner_odd for p in ((i, i + 1), (i + 1, i))]
    relay = [p for i in inner_odd for p in ((i - 1, i + 1), (i + 2, i))]
    down = [(i, i + tile_cols) for i in spots if i + tile_cols < space_size]
    up = [(j, i) for i, j in down]
    vertical = [down + up] if tile_rows == 2 else [down, up]
    directions = len(vertical)
    swap = [(0, 1), (1, 0)]

    least, few = min(2, slots), min(3, slots)
    meta, wide_branch, tall_branch, q_here, q_send, kv_here, kv_send = pl.pallas_call(
        functools.partial(project_kernel, heads, least, few),
        in_specs=[HBM] * 7,
        out_specs=[SMEM] * 3 + [VMEM] * 4,
        out_shape=[
            jax.ShapeDtypeStruct((META,), jnp.int32),
            jax.ShapeDtypeStruct((1,), jnp.int32),
            jax.ShapeDtypeStruct((1,), jnp.int32),
            jax.ShapeDtypeStruct((heads, rows, HEAD_DIM), bf16),
            jax.ShapeDtypeStruct((slots, rows, HEAD_DIM), bf16),
            jax.ShapeDtypeStruct((heads, 2, rows, HEAD_DIM), bf16),
            jax.ShapeDtypeStruct((slots, 2, rows, HEAD_DIM), bf16),
        ],
        scratch_shapes=[
            pltpu.SMEM((2, heads), jnp.int32),
            pltpu.VMEM(tokens.shape, bf16),
            pltpu.VMEM(mod_shift.shape, f32),
            pltpu.VMEM(mod_scale.shape, f32),
            pltpu.VMEM(q_gain.shape, f32),
            pltpu.VMEM(k_gain.shape, f32),
            pltpu.VMEM((rows, feature_dim), bf16),
            pltpu.VMEM((3, feature_dim, inner), bf16),
            pltpu.SemaphoreType.DMA((6,)),
            pltpu.SemaphoreType.DMA((3,)),
        ],
        compiler_params=params(24),
        name="project",
    )(*[
        pltpu.with_memory_space_constraint(x, pltpu.HBM)
        for x in (windows.T, tokens, mod_shift, mod_scale, w_qkv, q_gain, k_gain)
    ])

    back = [[(j, i) for i, j in pairs] for pairs in vertical]
    lanes = 128
    stat_rows = 256

    def along_row(sent, asked, *operands):
        return row_step(sent, asked, *operands)

    def row_step(sent, asked, kv_send, kv_here, q_send, q_here, meta):
        parts = 2 if sent > few else 1
        each = 2 // parts
        packed = [kv_send[:sent, j * each : (j + 1) * each] for j in range(parts)]
        kv_other = lax.ppermute(kv_here, "tm", swap)
        near = [lax.ppermute(packed[0], "space", pair)]
        q_visit = jnp.stack([lax.ppermute(q_send[:asked], "space", pairs) for pairs in vertical])
        far_part = lax.ppermute(packed[-1], "space", far)
        if parts == 2:
            near.append(lax.ppermute(packed[1], "space", pair))
            near.append(lax.ppermute(near[0], "space", relay))
        near.append(far_part)
        near = [x for part in near for x in (part, lax.ppermute(part, "tm", swap))]
        if parts == 2:
            near = [near[i] for i in (0, 2, 1, 3, 4, 6, 5, 7)]
        o_own, lse_own, bias_own, bias_near = pl.pallas_call(
            functools.partial(own_tile_kernel, heads, tile_cols),
            in_specs=[SMEM] * 2 + [VMEM] * 3,
            out_specs=[VMEM] * 4,
            out_shape=[
                jax.ShapeDtypeStruct((heads, rows, HEAD_DIM), f32),
                jax.ShapeDtypeStruct((rows, lanes), f32),
                jax.ShapeDtypeStruct((rows, 2 * rows), f32),
                jax.ShapeDtypeStruct((rows, 4 * rows), f32),
            ],
            compiler_params=params(12),
            cost_estimate=pl.CostEstimate(
                flops=8 * heads * rows * rows * HEAD_DIM, bytes_accessed=6 << 20, transcendentals=2 * heads * rows * rows
            ),
            name="own_tile",
        )(frame_lists, frame_valid, q_here, kv_here, kv_other)
        o_near, lse_near, o_visit, lse_visit = pl.pallas_call(
            functools.partial(attend_kernel, parts),
            in_specs=[SMEM] + [VMEM] * (6 + len(near)),
            out_specs=[VMEM] * 4,
            out_shape=[
                jax.ShapeDtypeStruct((slots, rows, HEAD_DIM), f32),
                jax.ShapeDtypeStruct((rows, lanes), f32),
                jax.ShapeDtypeStruct((directions, slots, rows, HEAD_DIM), bf16),
                jax.ShapeDtypeStruct((directions, 8, stat_rows), f32),
            ],
            scratch_shapes=[pltpu.VMEM((stat_rows, lanes), f32)],
            compiler_params=params(24),
            name="attend",
        )(meta, q_here, q_visit, kv_here, kv_other, *near, bias_own, bias_near)
        return o_own, lse_own, o_near, lse_near, o_visit, lse_visit

    ways = [(n, asked) for n in range(least, slots + 1) for asked in ((few, slots) if n == least else (slots,))]
    o_own, lse_own, o_near, lse_near, o_visit, lse_visit = branch_on(
        wide_branch.reshape(()),
        [functools.partial(along_row, *way) for way in ways],
        kv_send, kv_here, q_send, q_here, meta,
    )

    def between_rows(sent, *operands):
        return return_step(sent, *operands)

    def return_step(sent, o_own, lse_own, o_near, lse_near, o_visit, lse_visit, meta):
        o_back = jnp.stack([lax.ppermute(o_visit[d, :sent], "space", back[d]) for d in range(directions)])
        lse_back = jnp.stack([lax.ppermute(lse_visit[d], "space", back[d]) for d in range(directions)])
        row = pl.pallas_call(
            functools.partial(row_kernel, heads),
            in_specs=[SMEM] + [VMEM] * 4,
            out_specs=[VMEM] * 3,
            out_shape=[
                jax.ShapeDtypeStruct((heads, rows, HEAD_DIM), f32),
                jax.ShapeDtypeStruct((rows, lanes), f32),
                jax.ShapeDtypeStruct((rows, inner), bf16),
            ],
            compiler_params=params(8),
            cost_estimate=pl.CostEstimate(flops=1 << 22, bytes_accessed=2 << 20, transcendentals=1 << 14),
            name="row_merge",
        )(meta, o_own, lse_own, o_near, lse_near)
        return pl.pallas_call(
            functools.partial(output_kernel, tile_cols, tile_rows),
            in_specs=[SMEM] + [VMEM] * 8,
            out_specs=HBM,
            out_shape=pltpu.HBM(tokens.shape, bf16),
            scratch_shapes=[
                pltpu.VMEM((rows, inner), bf16),
                pltpu.VMEM((lanes, stat_rows), f32),
                pltpu.VMEM(tokens.shape, bf16),
                pltpu.SemaphoreType.DMA((3,)),
            ],
            compiler_params=params(16),
            name="output",
        )(meta, tokens, mod_gate, w_out, *row, o_back, lse_back)

    mixed = branch_on(
        tall_branch.reshape(()),
        [functools.partial(between_rows, n) for n in range(least, slots + 1)],
        o_own, lse_own, o_near, lse_near, o_visit, lse_visit, meta,
    )
    return jnp.transpose(mixed, (1, 0, 2))[:, None]


def solution(mesh):
    in_specs = (
        P(("clips", "tm"), "space", None, None),
        P("clips"),
        P("clips"),
        P("clips"),
        P(),
        P(),
        P(),
        P(),
        P(),
        P("clips", None),
        P("clips"),
    )
    out_specs = P(("clips", "tm"), "space", None, None)
    return jax.shard_map(
        per_device, mesh=mesh, in_specs=in_specs, out_specs=out_specs, check_vma=False
    )
```
